128 devices in a mesh: ctx: 16 (over y, z_hi, core), tp: 8 (over z_lo, x).
Axes of the slice: x: 4, y: 4, z: 4 (z_hi: 2, z_lo: 2; z = z_hi * 2 + z_lo), core: 2. Of those that a mesh axis runs over, the one named last changes fastest.
Arguments:
- prompt_states: bfloat16 [2048, 1024], P('ctx'), may hold values from -1.5 to 1.5
- segment_ids: int32 [2048], P('ctx'), may hold values from 0 to 3, never falling along the last dimension, each value on 1 to 1024 neighbouring positions
- past_keys: bfloat16 [2048, 1024], P('ctx', 'tp'), may hold values from -1024 to 1024
- past_values: bfloat16 [2048, 1024], P('ctx', 'tp'), may hold values from -6 to 6
- cache_request: int32 [2048], P('ctx'), may hold values from 0 to 2, as said below
- decode_ids: int32 [4], replicated, may hold values from 0 to 32127
- embed_table: bfloat16 [32128, 1024], P(('ctx', 'tp')), may hold values from -6 to 6
- attn_gain: bfloat16 [1024], replicated, may hold values from 0.25 to 1.75
- ff_gain: bfloat16 [1024], replicated, may hold values from 0.25 to 1.75
- final_gain: bfloat16 [1024], replicated, may hold values from 0.25 to 1.75
- w_query: bfloat16 [1024, 1024], P(None, 'tp'), may hold values from -0.1875 to 0.1875
- w_key: bfloat16 [1024, 1024], P(None, 'tp'), may hold values from -0.1875 to 0.1875
- w_value: bfloat16 [1024, 1024], P(None, 'tp'), may hold values from -0.1875 to 0.1875
- w_out: bfloat16 [1024, 1024], P('tp'), may hold values from -0.1875 to 0.1875
- w_gate: bfloat16 [1024, 2816], P(None, 'tp'), may hold values from -0.1875 to 0.1875
- w_up: bfloat16 [1024, 2816], P(None, 'tp'), may hold values from -0.1875 to 0.1875
- w_down: bfloat16 [2816, 1024], P('tp'), may hold values from -0.109375 to 0.109375
- lm_head: bfloat16 [1024, 32128], P(None, ('ctx', 'tp')), may hold values from -0.1875 to 0.1875
Outputs:
- prompt_out: bfloat16 [2048, 1024], P('ctx')
- logits: float32 [4, 32128], P(None, ('ctx', 'tp'))
- relaid_keys: bfloat16 [2048, 1024], P(('ctx', 'tp'))
- relaid_values: bfloat16 [2048, 1024], P(('ctx', 'tp'))
The draws below stay inside these ranges and needn't reach their ends.
Inputs may be any that keep to these rules, and one draw needn't show every extreme that they name: `cache_request`: only the even requests have cached rows, which may lie on any devices. `segment_ids`: the tokens of a request are consecutive; a request holds at most 1024 of them, and one request holds exactly that many.
All inputs are finite; a program needn't handle non-finite values.
Results may differ from the reference program's by a relative error of at most 0.03.
Values may be sent and summed in bfloat16 or wider, within the bound.
A program may use at most 64 MiB of HBM per device.

```python
import math
import jax
import jax.numpy as jnp
import numpy as np
from jax import lax

D = 1024
H = 16
DH = 64
FF = 2816
VOCAB = 32128
REQS = 4
TOKENS = 2048
CACHE = 2048


def draw_cache_request(key, part):
    return 2 * jax.random.randint(key, (CACHE,), 0, REQS // 2, dtype=jnp.int32)


def draw_past_keys(key, part):
    base_key = jax.random.fold_in(key, 11)
    normal = jnp.clip(jax.random.normal(base_key, (CACHE, H * DH), jnp.float32), -6.0, 6.0)
    return normal.astype(jnp.bfloat16)


def place_ends(values, rng, smallest, largest):
    index_at = [jax.random.randint(jax.random.fold_in(rng, axis), (), 0, length) for axis, length in enumerate(values.shape)]
    widest = values.shape.index(max(values.shape))
    neighbour = index_at[:widest] + [(index_at[widest] + 1) % values.shape[widest]] + index_at[widest + 1:]
    return values.at[tuple(index_at)].set(smallest).at[tuple(neighbour)].set(largest)


def steps_of(own_key, extent, pieces, smallest, largest):
    level, own = 1.0, jax.random.fold_in(own_key, 6)
    for axis_at, shards_of in pieces:
        draws = jnp.exp(jax.random.uniform(jax.random.fold_in(own, axis_at), (shards_of,), jnp.float32, smallest / len(pieces), largest / len(pieces)))
        level = level * jnp.repeat(draws, extent[axis_at] // shards_of).reshape([-1 if axis == axis_at else 1 for axis in range(len(extent))])
    return level


def length_profile(count, total, reach, skew):
    portions = [(1 << 20) // math.isqrt(grade ** skew) + 1 for grade in range(2, count + 1)]
    rest, counts = total - reach - (count - 1), [1] * (count - 1)
    while rest > 0:
        movable = [i for i in range(count - 1) if counts[i] < reach]
        mass, left = sum([portions[i] for i in movable]), rest
        for i in movable:
            addition = min(reach - counts[i], max(1, left * portions[i] // mass), rest)
            counts[i] = counts[i] + addition
            rest = rest - addition
    return np.array([reach] + counts)


def uneven(rng, number_of, total, bound, lean):
    if number_of == 2:
        one = jax.random.randint(rng, (), max(1, total - bound), min(bound, total - 1) + 1)
        return jnp.stack([one, total - one])
    sizes = jnp.asarray(length_profile(number_of, total, bound, lean), jnp.int32)
    couples = (number_of - 1) // 2
    source_of, taker = sizes[1:1 + 2 * couples:2], sizes[2:2 + 2 * couples:2]
    margin = jnp.minimum(source_of - 1, bound - taker)
    moved = jax.random.randint(jax.random.fold_in(rng, 1), (couples,), 0, 1 << 20) % (margin + 1)
    sizes = sizes.at[1:1 + 2 * couples:2].set(source_of - moved).at[2:2 + 2 * couples:2].set(taker + moved)
    return sizes[jax.random.permutation(jax.random.fold_in(rng, 2), number_of)]


def scatter_about(key, extent, scale, bound, split=(), held_as=jnp.bfloat16):
    level = steps_of(key, extent, split, -0.22, 0.18) if split else 1.0
    drawn = jax.random.normal(key, extent, jnp.float32) * scale * level
    return jnp.minimum(jnp.maximum(drawn, -bound), bound).astype(held_as)


def setup_inputs(seed: int = 0) -> dict:
    key_list = jax.random.split(jax.random.key(seed), 19)
    return {
        "prompt_states": scatter_about(key_list[0], (TOKENS, D), 0.1, 1.5, ((0, 16),)),
        "segment_ids": jnp.searchsorted(jnp.cumsum(uneven(key_list[1], REQS, TOKENS, TOKENS // 2, 2)), jnp.arange(TOKENS), side="right").astype(jnp.int32),
        "past_keys": draw_past_keys(jax.random.fold_in(key_list[18], 71), 0),
        "past_values": scatter_about(key_list[3], (CACHE, H * DH), 1.0, 6.0, ((0, 16), (1, 8))),
        "cache_request": draw_cache_request(jax.random.fold_in(key_list[18], 71), 0),
        "decode_ids": place_ends(jax.random.randint(key_list[5], (REQS,), 0, VOCAB), jax.random.fold_in(key_list[5], 1), 0, VOCAB - 1).astype(jnp.int32),
        "embed_table": scatter_about(key_list[6], (VOCAB, D), 1.0, 6.0, ((0, 128),)),
        "attn_gain": jnp.clip(1.0 + 0.15 * jax.random.normal(key_list[7], (D,), jnp.float32), 0.25, 1.75).astype(jnp.bfloat16),
        "ff_gain": jnp.clip(1.0 + 0.15 * jax.random.normal(key_list[8], (D,), jnp.float32), 0.25, 1.75).astype(jnp.bfloat16),
        "final_gain": jnp.clip(1.0 + 0.15 * jax.random.normal(key_list[9], (D,), jnp.float32), 0.25, 1.75).astype(jnp.bfloat16),
        "w_query": scatter_about(key_list[10], (D, H * DH), D ** -0.5, 0.1875, ((1, 8),)),
        "w_key": scatter_about(key_list[11], (D, H * DH), D ** -0.5, 0.1875, ((1, 8),)),
        "w_value": scatter_about(key_list[12], (D, H * DH), D ** -0.5, 0.1875, ((1, 8),)),
        "w_out": scatter_about(key_list[13], (H * DH, D), (H * DH) ** -0.5, 0.1875, ((0, 8),)),
        "w_gate": scatter_about(key_list[14], (D, FF), D ** -0.5, 0.1875, ((1, 8),)),
        "w_up": scatter_about(key_list[15], (D, FF), D ** -0.5, 0.1875, ((1, 8),)),
        "w_down": scatter_about(key_list[16], (FF, D), FF ** -0.5, 0.109375, ((0, 8),)),
        "lm_head": scatter_about(key_list[17], (D, VOCAB), D ** -0.5, 0.1875, ((1, 128),)),
    }


epsilon = 1e-06
scale_factor = 0.125
negative = -1e+30

def rms_norm(states, gain):
    states = states.astype(jnp.float32)
    mean_square = lax.optimization_barrier(jnp.mean(states * states, axis=-1, keepdims=True))
    return (states * lax.rsqrt(mean_square + epsilon) * gain.astype(jnp.float32)).astype(jnp.bfloat16)

def partial_attend(queries, keys, values, allowed):
    scores = jnp.einsum('qhd,khd->qhk', queries.astype(jnp.float32), keys.astype(jnp.float32)) * scale_factor
    scores = jnp.where(allowed[:, None, :], scores, negative)
    highest = lax.optimization_barrier(jnp.max(scores, axis=2))
    weights = jnp.where(allowed[:, None, :], jnp.exp(scores - highest[:, :, None]), 0.0)
    weight_sum = lax.optimization_barrier(jnp.sum(weights, axis=2))
    summed = jnp.einsum('qhk,khd->qhd', weights.astype(jnp.bfloat16).astype(jnp.float32), values.astype(jnp.float32))
    return (highest, weight_sum, summed)

def gated_units(normed, w_gate, w_up, w_down):
    gate_value = jnp.dot(normed, w_gate, preferred_element_type=jnp.float32)
    up_value = jnp.dot(normed, w_up, preferred_element_type=jnp.float32)
    hidden = (jax.nn.gelu(gate_value, approximate=True) * up_value).astype(jnp.bfloat16)
    return jnp.dot(hidden, w_down, preferred_element_type=jnp.float32)

def project(normed, weight):
    return jnp.dot(normed, weight, preferred_element_type=jnp.float32).astype(jnp.bfloat16)

def reference(prompt_states, segment_ids, past_keys, past_values, cache_request, decode_ids, embed_table, attn_gain, ff_gain, final_gain, w_query, w_key, w_value, w_out, w_gate, w_up, w_down, lm_head):
    normed = rms_norm(prompt_states, attn_gain)
    queries = project(normed, w_query).reshape(TOKENS, H, DH)
    keys = project(normed, w_key)
    values = project(normed, w_value)
    all_keys = jnp.concatenate([keys.reshape(TOKENS, H, DH), past_keys.reshape(CACHE, H, DH)], axis=0)
    all_values = jnp.concatenate([values.reshape(TOKENS, H, DH), past_values.reshape(CACHE, H, DH)], axis=0)
    key_segment = jnp.concatenate([segment_ids, cache_request]).astype(jnp.int32)
    key_position = jnp.concatenate([jnp.arange(TOKENS, dtype=jnp.int32), jnp.full((CACHE,), -1, jnp.int32)])
    query_block = math.gcd(TOKENS, 256)

    def one_block(block_index):
        first_row = (block_index * query_block).astype(jnp.int32)
        block_queries = lax.dynamic_slice_in_dim(queries, first_row, query_block, 0)
        segment = lax.dynamic_slice_in_dim(segment_ids, first_row, query_block, 0)
        positions = first_row + jnp.arange(query_block, dtype=jnp.int32)
        allowed = (segment[:, None] == key_segment[None, :]) & (key_position[None, :] <= positions[:, None])
        highest, weight_sum, summed = partial_attend(block_queries, all_keys, all_values, allowed)
        return (summed / weight_sum[:, :, None]).astype(jnp.bfloat16)
    attended = lax.map(one_block, jnp.arange(TOKENS // query_block, dtype=jnp.int32)).reshape(TOKENS, H * DH)
    residual = prompt_states.astype(jnp.float32) + jnp.dot(attended, w_out, preferred_element_type=jnp.float32)
    prompt_out = (residual + gated_units(rms_norm(residual, ff_gain), w_gate, w_up, w_down)).astype(jnp.bfloat16)
    embedded = jnp.take(embed_table, decode_ids, axis=0)
    decode_normed = rms_norm(embedded, attn_gain)
    decode_queries = project(decode_normed, w_query).reshape(REQS, H, DH)
    decode_keys = project(decode_normed, w_key).reshape(REQS, H, DH)
    decode_values = project(decode_normed, w_value).reshape(REQS, H, DH)
    every_key = jnp.concatenate([all_keys, decode_keys], axis=0)
    every_value = jnp.concatenate([all_values, decode_values], axis=0)
    every_segment = jnp.concatenate([key_segment, jnp.arange(REQS, dtype=jnp.int32)])
    requests = jnp.arange(REQS, dtype=jnp.int32)
    allowed = requests[:, None] == every_segment[None, :]
    highest, weight_sum, summed = partial_attend(decode_queries, every_key, every_value, allowed)
    decode_attended = (summed / weight_sum[:, :, None]).astype(jnp.bfloat16).reshape(REQS, H * DH)
    decode_residual = embedded.astype(jnp.float32) + jnp.dot(decode_attended, w_out, preferred_element_type=jnp.float32)
    decode_final = decode_residual + gated_units(rms_norm(decode_residual, ff_gain), w_gate, w_up, w_down)
    logits = jnp.dot(rms_norm(decode_final, final_gain), lm_head, preferred_element_type=jnp.float32)
    return (prompt_out, logits, keys, values)
```

```python
import jax
import jax.numpy as jnp
from jax import lax
from jax.experimental import pallas as pl
from jax.experimental.pallas import tpu as pltpu
from jax.sharding import PartitionSpec as P

DH = 64
EPS = 1e-06
NEG = -1e30
FLOOR = -1e29
MESH = pl.DeviceIdType.MESH
F32 = jnp.float32
BF16 = jnp.bfloat16


def dot(a, b):
    return jnp.dot(a, b, preferred_element_type=F32)


def dot_nt(a, b):
    return lax.dot_general(a, b, (((1,), (1,)), ((), ())), preferred_element_type=F32)


def norm(states, gain):
    mean_square = jnp.mean(states * states, axis=-1, keepdims=True)
    return (states * lax.rsqrt(mean_square + EPS) * gain).astype(BF16)


def kernel(
    ids_ref, x_hbm, seg_hbm, pk_hbm, pv_hbm, creq_hbm, emb_hbm,
    ag_hbm, fg_hbm, lg_hbm, wq_hbm, wk_hbm, wv_hbm, wo_hbm, wg_hbm, wu_hbm, wd_hbm, lm_hbm,
    out_ref, logits_ref, relk_ref, relv_ref,
    x_v, ag_v, fg_v, lg_v, wq_v, wk_v, wv_v, wo_v, wg_v, wu_v, wd_v, lm_v, emb_v, pv_v,
    idown, vrow, kid_s, s_s, p_s, osend, stsend, dsend, part_s, nbuf, decp_s, e1src, e2src, fin_s,
    kbuf, vtbuf, qbuf, idy, idz, obuf, stbuf, dbuf, e1buf, e2buf, rs1buf, ar1buf, rs2buf, ar2buf,
    lsem, ksend, krecv, qsend, qrecv, isend, irecv, e1send, e1recv, e2send, e2recv,
    rlsend, rlrecv, osems, orecv, dsems, drecv, tsend, trecv,
):
    c = lax.axis_index("ctx")
    t = lax.axis_index("tp")
    y = lax.div(c, 4)
    zc = lax.rem(c, 4)

    def ypeer(d):
        return (lax.rem(y + d, 4) * 4 + zc, t)

    def zpeer(e):
        return (y * 4 + lax.rem(zc + e, 4), t)

    def tpeer(r):
        return (c, lax.rem(t + r, 8))

    def cpeer(k):
        return (lax.rem(c + k, 16), t)

    def remote(src, dst, ssem, rsem, peer):
        return pltpu.make_async_remote_copy(
            src_ref=src, dst_ref=dst, send_sem=ssem, recv_sem=rsem,
            device_id=peer, device_id_type=MESH,
        )

    barrier = pltpu.get_barrier_semaphore()
    for k in range(1, 16):
        pl.semaphore_signal(barrier, 1, device_id=cpeer(k), device_id_type=MESH)
    for r in range(1, 8):
        pl.semaphore_signal(barrier, 1, device_id=tpeer(r), device_id_type=MESH)

    loads = {}
    todo = [
        ("x", x_hbm, x_v), ("ag", ag_hbm, ag_v), ("wk", wk_hbm, wk_v), ("wv", wv_hbm, wv_v),
        ("wq", wq_hbm, wq_v), ("pk", pk_hbm, kbuf.at[pl.ds(128, 128)]), ("pv", pv_hbm, pv_v),
        ("seg", seg_hbm, idown.at[0]), ("creq", creq_hbm, idown.at[1]),
        ("emb", emb_hbm, emb_v), ("wo", wo_hbm, wo_v), ("fg", fg_hbm, fg_v),
        ("wg", wg_hbm, wg_v), ("wu", wu_hbm, wu_v), ("wd", wd_hbm, wd_v),
        ("lg", lg_hbm, lg_v), ("lm", lm_hbm, lm_v),
    ]
    for i, (name, src, dst) in enumerate(todo):
        loads[name] = pltpu.make_async_copy(src, dst, lsem.at[i])
        loads[name].start()

    def gain_of(ref):
        return ref[...].astype(F32).reshape(1, 1024)

    loads["x"].wait()
    loads["ag"].wait()
    a_gain = gain_of(ag_v)
    normed = norm(x_v[...].astype(F32), a_gain)
    loads["wk"].wait()
    kbuf[0:128, :] = dot(normed, wk_v[...]).astype(BF16)
    loads["wv"].wait()
    values = dot(normed, wv_v[...])
    vrow[...] = values.astype(BF16)
    vtbuf[:, 0:128] = values.T.astype(BF16)
    loads["wq"].wait()
    queries = dot(normed, wq_v[...]).astype(BF16).astype(F32) * 0.125
    qbuf[0] = queries.T.astype(BF16)
    loads["pk"].wait()
    loads["pv"].wait()
    vtbuf[:, 128:256] = pv_v[...].astype(F32).T.astype(BF16)
    loads["seg"].wait()
    loads["creq"].wait()

    first_row = (c * 8 + t) * 251
    row16 = lax.broadcasted_iota(jnp.int32, (16, 251), 0)
    col16 = lax.broadcasted_iota(jnp.int32, (16, 251), 1) + first_row
    wanted = jnp.full((16, 251), -1, jnp.int32)
    for q in range(4):
        wanted = jnp.where(row16 == q, ids_ref[q], wanted)
    one_hot = (col16 == wanted).astype(F32).astype(BF16)
    loads["emb"].wait()
    e1src[...] = dot(one_hot, emb_v[...])[0:4].astype(BF16)

    pl.semaphore_wait(barrier, 22)

    kv_copies = []
    for d in range(1, 4):
        kv_copies.append(remote(
            kbuf.at[pl.ds(0, 256)], kbuf.at[pl.ds(256 * d, 256)],
            ksend.at[d, 0], krecv.at[d, 0], ypeer(d)))
        kv_copies.append(remote(
            vtbuf.at[:, pl.ds(0, 256)], vtbuf.at[:, pl.ds(256 * d, 256)],
            ksend.at[d, 1], krecv.at[d, 1], ypeer(d)))
        kv_copies.append(remote(idown, idy.at[d], isend.at[0, d], irecv.at[0, d], ypeer(d)))
    q_copies = []
    for e in range(1, 4):
        q_copies.append(remote(qbuf.at[0], qbuf.at[e], qsend.at[e], qrecv.at[e], zpeer(e)))
        q_copies.append(remote(idown, idz.at[e], isend.at[1, e], irecv.at[1, e], zpeer(e)))
    for copy in kv_copies + q_copies:
        copy.start()
    e1_copies = []
    for k in range(1, 16):
        e1_copies.append(remote(e1src, e1buf.at[k], e1send.at[k], e1recv.at[k], cpeer(k)))
    for copy in e1_copies:
        copy.start()

    my_columns = pl.ds(pl.multiple_of(t * 128, 128), 128)
    my_rows = pl.ds(pl.multiple_of(t * 16, 16), 16)
    rel_copies = []
    for r in range(1, 8):
        other = pl.ds(pl.multiple_of(lax.rem(t + r, 8) * 16, 16), 16)
        rel_copies.append(remote(
            kbuf.at[other], relk_ref.at[:, my_columns], rlsend.at[0, r], rlrecv.at[0, r], tpeer(r)))
        rel_copies.append(remote(
            vrow.at[other], relv_ref.at[:, my_columns], rlsend.at[1, r], rlrecv.at[1, r], tpeer(r)))
    for copy in rel_copies:
        copy.start()
    relk_ref[:, my_columns] = kbuf[my_rows, :]
    relv_ref[:, my_columns] = vrow[my_rows, :]

    total = e1src[...].astype(F32)
    for k in range(1, 16):
        e1_copies[k - 1].wait()
        total = total + e1buf[k].astype(F32)
    e2src[...] = total.astype(BF16)
    e2_copies = []
    for r in range(1, 8):
        e2_copies.append(remote(e2src, e2buf.at[r], e2send.at[r], e2recv.at[r], tpeer(r)))
        e2_copies[-1].start()

    for copy in kv_copies:
        copy.wait()
    idy[0] = idown[...]
    idz[0] = idown[...]
    id_rows = []
    for d in range(4):
        id_rows.append(idy[d, 0:1, :].astype(F32))
        id_rows.append(idy[d, 1:2, :].astype(F32))
    id_columns = jnp.concatenate(id_rows + [jnp.zeros((120, 128), F32)], axis=0).T
    for b in range(8):
        kid_s[b] = jnp.broadcast_to(id_columns[:, b : b + 1], (128, 128))
    for copy in q_copies:
        copy.wait()

    k_iota = lax.broadcasted_iota(jnp.int32, (128, 128), 0)
    q_iota = lax.broadcasted_iota(jnp.int32, (128, 128), 1)

    def attend(i, _):
        e = lax.rem(i + 1, 4)
        qt = qbuf[e]
        top = qt[0:64, :]
        low = qt[64:128, :]
        zero = jnp.zeros((64, 128), BF16)
        qd = jnp.concatenate(
            [jnp.concatenate([top, zero], axis=1), jnp.concatenate([zero, low], axis=1)], axis=0)
        qid = idz[e, 0:1, :].astype(F32)
        q_at = y * 512 + lax.rem(zc - e + 4, 4) * 128
        highest = jnp.full((8, 256), FLOOR, F32)
        for b in range(8):
            s = dot(kbuf[b * 128 : (b + 1) * 128, :], qd)
            ok = kid_s[b] == qid
            if b % 2 == 0:
                k_at = lax.rem(y - b // 2 + 4, 4) * 512 + zc * 128
                ok = ok & (k_iota + (k_at - q_at) <= q_iota)
            s = jnp.where(jnp.concatenate([ok, ok], axis=1), s, NEG)
            s_s[b * 128 : (b + 1) * 128, :] = s
            highest = jnp.maximum(highest, jnp.max(s.reshape(16, 8, 256), axis=0))
        m = jnp.max(highest, axis=0, keepdims=True)
        total_w = jnp.zeros((8, 256), F32)
        for b in range(8):
            w = jnp.exp(s_s[b * 128 : (b + 1) * 128, :] - m)
            total_w = total_w + jnp.sum(w.reshape(16, 8, 256), axis=0)
            p_s[b * 128 : (b + 1) * 128, :] = w.astype(BF16)
        l = jnp.sum(total_w, axis=0, keepdims=True)
        o = dot(vtbuf[...], p_s[...])
        f = lax.rem(4 - e, 4)
        osend[f] = jnp.concatenate([o[0:64, 0:128], o[64:128, 128:256]], axis=0).astype(BF16)
        stsend[f] = jnp.concatenate(
            [m[:, 0:128], m[:, 128:256], l[:, 0:128], l[:, 128:256], jnp.zeros((4, 128), F32)],
            axis=0)

        @pl.when(i < 3)
        def _():
            remote(osend.at[f], obuf.at[f], osems.at[0, f], orecv.at[0, f], zpeer(f)).start()
            remote(stsend.at[f], stbuf.at[f], osems.at[1, f], orecv.at[1, f], zpeer(f)).start()

        return 0

    lax.fori_loop(0, 4, attend, 0)
    obuf[0] = osend[0]
    stbuf[0] = stsend[0]

    total = e2src[...].astype(F32)
    for r in range(1, 8):
        e2_copies[r - 1].wait()
        total = total + e2buf[r].astype(F32)
    embedded = total
    d_normed = jnp.concatenate(
        [norm(embedded, a_gain).astype(F32), jnp.zeros((12, 1024), F32)], axis=0).astype(BF16)
    dq = dot(d_normed, wq_v[...]).astype(BF16).astype(F32)[0:4] * 0.125
    dk = dot(d_normed, wk_v[...]).astype(BF16).astype(F32)[0:4]
    dv = dot(d_normed, wv_v[...]).astype(BF16).astype(F32)[0:4]
    lane4 = lax.broadcasted_iota(jnp.int32, (4, 128), 1)
    qd8 = jnp.concatenate(
        [jnp.where(lane4 < 64, dq, 0.0), jnp.where(lane4 >= 64, dq, 0.0)], axis=0)
    qd16 = jnp.concatenate([qd8, jnp.zeros((8, 128), F32)], axis=0).astype(BF16)
    k_ids = jnp.concatenate(id_rows, axis=1)
    rid = (lax.broadcasted_iota(jnp.int32, (16, 1024), 0) % 4).astype(F32)
    s = jnp.where(rid == k_ids, dot_nt(qd16, kbuf[...]), NEG)
    m = jnp.maximum(jnp.max(s, axis=1, keepdims=True), FLOOR)
    w = jnp.exp(s - m)
    l = jnp.sum(w, axis=1, keepdims=True)
    o = dot_nt(w.astype(BF16), vtbuf[...])
    dsend[0:8, :] = o[0:8]
    dsend[8:16, :] = jnp.broadcast_to(m[0:8], (8, 128))
    dsend[16:24, :] = jnp.broadcast_to(l[0:8], (8, 128))
    d_copies = []
    for e in range(1, 4):
        d_copies.append(remote(dsend, dbuf.at[e], dsems.at[e], drecv.at[e], zpeer(e)))
        d_copies[-1].start()

    for f in range(1, 4):
        remote(osend.at[f], obuf.at[f], osems.at[0, f], orecv.at[0, f], zpeer(f)).wait()
        remote(stsend.at[f], stbuf.at[f], osems.at[1, f], orecv.at[1, f], zpeer(f)).wait()
    stats = [stbuf[f] for f in range(4)]
    tops = [st[0:2] for st in stats]
    joint = jnp.maximum(jnp.maximum(tops[0], tops[1]), jnp.maximum(tops[2], tops[3]))
    scales = [jnp.exp(tp_ - joint) for tp_ in tops]
    weight = sum(sc * st[2:4] for sc, st in zip(scales, stats))
    inverse = 1.0 / weight
    attended = jnp.zeros((128, 128), F32)
    for f in range(4):
        factor = scales[f] * inverse
        spread = jnp.concatenate(
            [jnp.broadcast_to(factor[0:1], (64, 128)), jnp.broadcast_to(factor[1:2], (64, 128))],
            axis=0)
        attended = attended + obuf[f].astype(F32) * spread
    loads["wo"].wait()
    head_term = dot(attended.T.astype(BF16), wo_v[...])
    part_s[...] = head_term.astype(BF16)
    rs1_copies = []
    for r in range(1, 8):
        other = pl.ds(pl.multiple_of(lax.rem(t + r, 8) * 16, 16), 16)
        rs1_copies.append(remote(
            part_s.at[other], rs1buf.at[r], tsend.at[0, r], trecv.at[0, r], tpeer(r)))
        rs1_copies[-1].start()

    own_m = jnp.sum(qd8 * jnp.concatenate([dk, dk], axis=0), axis=1, keepdims=True)
    own_m = jnp.broadcast_to(own_m, (8, 128))
    for copy in d_copies:
        copy.wait()
    dparts = [dsend[...]] + [dbuf[e] for e in range(1, 4)]
    joint = own_m
    for part in dparts:
        joint = jnp.maximum(joint, part[8:16])
    own_scale = jnp.exp(own_m - joint)
    weight = own_scale
    summed = own_scale * jnp.concatenate([dv, dv], axis=0)
    for part in dparts:
        scale = jnp.exp(part[8:16] - joint)
        weight = weight + scale * part[16:24]
        summed = summed + scale * part[0:8]
    summed = summed / weight
    d_attended = jnp.where(lane4 < 64, summed[0:4], summed[4:8])
    d_attended = jnp.concatenate([d_attended, jnp.zeros((12, 128), F32)], axis=0).astype(BF16)
    d_term = dot(d_attended, wo_v[...])[0:4]
    decp_s[0] = d_term.astype(BF16)
    ar1_copies = []
    for r in range(1, 8):
        ar1_copies.append(remote(
            decp_s.at[0], ar1buf.at[r], tsend.at[1, r], trecv.at[1, r], tpeer(r)))
        ar1_copies[-1].start()

    residual = x_v[my_rows, :].astype(F32) + part_s[my_rows, :].astype(F32)
    for r in range(1, 8):
        rs1_copies[r - 1].wait()
        residual = residual + rs1buf[r].astype(F32)
    loads["fg"].wait()
    f_gain = gain_of(fg_v)
    nbuf[my_rows, :] = norm(residual, f_gain)
    ag1_copies = []
    for r in range(1, 8):
        ag1_copies.append(remote(
            nbuf.at[my_rows], nbuf.at[my_rows], tsend.at[2, r], trecv.at[2, r], tpeer(r)))
        ag1_copies[-1].start()
    fin_s[...] = residual

    d_residual = embedded + decp_s[0].astype(F32)
    for r in range(1, 8):
        ar1_copies[r - 1].wait()
        d_residual = d_residual + ar1buf[r].astype(F32)
    nbuf[128:144, :] = jnp.concatenate(
        [norm(d_residual, f_gain).astype(F32), jnp.zeros((12, 1024), F32)], axis=0).astype(BF16)

    loads["wg"].wait()
    loads["wu"].wait()
    loads["wd"].wait()
    for copy in ag1_copies:
        copy.wait()
    gate = dot(nbuf[...], wg_v[...])
    up = dot(nbuf[...], wu_v[...])
    hidden = (jax.nn.gelu(gate, approximate=True) * up).astype(BF16)
    unit_term = dot(hidden, wd_v[...])
    part_s[...] = unit_term[0:128].astype(BF16)
    decp_s[1] = unit_term[128:132].astype(BF16)
    rs2_copies = []
    for r in range(1, 8):
        other = pl.ds(pl.multiple_of(lax.rem(t + r, 8) * 16, 16), 16)
        rs2_copies.append(remote(
            part_s.at[other], rs2buf.at[r], tsend.at[3, r], trecv.at[3, r], tpeer(r)))
        rs2_copies[-1].start()
    ar2_copies = []
    for r in range(1, 8):
        ar2_copies.append(remote(
            decp_s.at[1], ar2buf.at[r], tsend.at[4, r], trecv.at[4, r], tpeer(r)))
        ar2_copies[-1].start()

    final = fin_s[...] + part_s[my_rows, :].astype(F32)
    for r in range(1, 8):
        rs2_copies[r - 1].wait()
        final = final + rs2buf[r].astype(F32)
    out_ref[my_rows, :] = final.astype(BF16)
    ag2_copies = []
    for r in range(1, 8):
        ag2_copies.append(remote(
            out_ref.at[my_rows], out_ref.at[my_rows], tsend.at[5, r], trecv.at[5, r], tpeer(r)))
        ag2_copies[-1].start()

    d_final = d_residual + decp_s[1].astype(F32)
    for r in range(1, 8):
        ar2_copies[r - 1].wait()
        d_final = d_final + ar2buf[r].astype(F32)
    loads["lg"].wait()
    loads["lm"].wait()
    l_normed = jnp.concatenate(
        [norm(d_final, gain_of(lg_v)).astype(F32), jnp.zeros((12, 1024), F32)], axis=0).astype(BF16)
    logits_ref[...] = dot(l_normed, lm_v[...])[0:4]

    for copy in rel_copies + ag2_copies:
        copy.wait()


def on_device(
    prompt_states, segment_ids, past_keys, past_values, cache_request, decode_ids, embed_table,
    attn_gain, ff_gain, final_gain, w_query, w_key, w_value, w_out, w_gate, w_up, w_down, lm_head,
):
    anywhere = pl.BlockSpec(memory_space=pl.ANY)
    vmem = pl.BlockSpec(memory_space=pltpu.VMEM)
    dma = pltpu.SemaphoreType.DMA
    local = [
        ((128, 1024), BF16), ((1024,), BF16), ((1024,), BF16), ((1024,), BF16),
        ((1024, 128), BF16), ((1024, 128), BF16), ((1024, 128), BF16), ((128, 1024), BF16),
        ((1024, 352), BF16), ((1024, 352), BF16), ((352, 1024), BF16), ((1024, 251), BF16),
        ((251, 1024), BF16), ((128, 128), BF16),
        ((8, 128), jnp.int32), ((128, 128), BF16), ((8, 128, 128), F32), ((1024, 256), F32),
        ((1024, 256), BF16), ((4, 128, 128), BF16), ((4, 8, 128), F32), ((24, 128), F32),
        ((128, 1024), BF16), ((144, 1024), BF16), ((2, 4, 1024), BF16), ((4, 1024), BF16),
        ((4, 1024), BF16), ((16, 1024), F32),
    ]
    arriving = [
        ((1024, 128), BF16), ((128, 1024), BF16), ((4, 128, 128), BF16), ((4, 8, 128), jnp.int32),
        ((4, 8, 128), jnp.int32), ((4, 128, 128), BF16), ((4, 8, 128), F32), ((4, 24, 128), F32),
        ((16, 4, 1024), BF16), ((8, 4, 1024), BF16), ((8, 16, 1024), BF16), ((8, 4, 1024), BF16),
        ((8, 16, 1024), BF16), ((8, 4, 1024), BF16),
    ]
    semaphores = [
        dma((17,)), dma((4, 2)), dma((4, 2)), dma((4,)), dma((4,)), dma((2, 4)), dma((2, 4)),
        dma((16,)), dma((16,)), dma((8,)), dma((8,)), dma((2, 8)), dma((2, 8)),
        dma((2, 4)), dma((2, 4)), dma((4,)), dma((4,)), dma((6, 8)), dma((6, 8)),
    ]
    return pl.pallas_call(
        kernel,
        out_shape=(
            jax.ShapeDtypeStruct((128, 1024), BF16),
            jax.ShapeDtypeStruct((4, 251), F32),
            jax.ShapeDtypeStruct((16, 1024), BF16),
            jax.ShapeDtypeStruct((16, 1024), BF16),
        ),
        in_specs=[pl.BlockSpec(memory_space=pltpu.SMEM)] + [anywhere] * 17,
        out_specs=(vmem, vmem, vmem, vmem),
        scratch_shapes=[pltpu.VMEM(s, d) for s, d in local + arriving] + semaphores,
        compiler_params=pltpu.CompilerParams(
            collective_id=0, has_side_effects=True, vmem_limit_bytes=48 * 1024 * 1024),
    )(
        decode_ids, prompt_states, segment_ids, past_keys, past_values, cache_request, embed_table,
        attn_gain, ff_gain, final_gain, w_query, w_key, w_value, w_out, w_gate, w_up, w_down,
        lm_head,
    )


def solution(mesh):
    placed = (
        P("ctx", None),
        P("ctx"),
        P("ctx", "tp"),
        P("ctx", "tp"),
        P("ctx"),
        P(),
        P(("ctx", "tp"), None),
        P(),
        P(),
        P(),
        P(None, "tp"),
        P(None, "tp"),
        P(None, "tp"),
        P("tp", None),
        P(None, "tp"),
        P(None, "tp"),
        P("tp", None),
        P(None, ("ctx", "tp")),
    )
    return jax.shard_map(
        on_device,
        mesh=mesh,
        in_specs=placed,
        out_specs=(
            P("ctx", None),
            P(None, ("ctx", "tp")),
            P(("ctx", "tp"), None),
            P(("ctx", "tp"), None),
        ),
        check_vma=False,
    )
```

```python
import jax
import jax.numpy as jnp
from jax import lax
from jax.experimental import pallas as pl
from jax.experimental.pallas import tpu as pltpu
from jax.sharding import PartitionSpec as P

DH = 64
EPS = 1e-06
NEG = -1e30
FLOOR = -1e29
MESH = pl.DeviceIdType.MESH
F32 = jnp.float32
BF16 = jnp.bfloat16


def dot(a, b):
    return jnp.dot(a, b, preferred_element_type=F32)


def dot_nt(a, b):
    return lax.dot_general(a, b, (((1,), (1,)), ((), ())), preferred_element_type=F32)


def norm(states, gain):
    mean_square = jnp.mean(states * states, axis=-1, keepdims=True)
    return (states * lax.rsqrt(mean_square + EPS) * gain).astype(BF16)


def kernel(
    ids_ref, x_hbm, seg_hbm, pk_hbm, pv_hbm, creq_hbm, emb_hbm,
    ag_hbm, fg_hbm, lg_hbm, wq_hbm, wk_hbm, wv_hbm, wo_hbm, wg_hbm, wu_hbm, wd_hbm, lm_hbm,
    out_ref, logits_ref, relk_ref, relv_ref,
    x_v, ag_v, fg_v, lg_v, qkv_v, wo_v, ffn_v, lm_v, emb_v, pv_v,
    vrow, kid_s, s_s, p_s, osend, stsend, part_s, nbuf, decp_s, fin_s,
    past, new, idall, qbuf, obuf, stbuf, dbuf, e1buf, e2buf, e3buf,
    rs1buf, ar1buf, rs2buf, ar2buf,
    lsem, ssem, rsem,
):
    c = lax.axis_index("ctx")
    t = lax.axis_index("tp")
    y = lax.div(c, 4)
    zc = lax.rem(c, 4)

    def ypeer(d):
        return (lax.rem(y + d, 4) * 4 + zc, t)

    def zpeer(e):
        return (y * 4 + lax.rem(zc + e, 4), t)

    def tpeer(r):
        return (c, lax.rem(t + r, 8))

    names = (
        "past", "new", "ids", "q", "e1", "e2", "e3", "relk", "relv", "part", "stats", "dpart",
        "rs1", "ar1", "ag1", "rs2", "ar2", "ag2",
    )

    def remote(name, src, dst, peer):
        at = names.index(name)
        return pltpu.make_async_remote_copy(
            src_ref=src, dst_ref=dst, send_sem=ssem.at[at], recv_sem=rsem.at[at],
            device_id=peer, device_id_type=MESH,
        )

    def arrived(name, whole):
        remote(name, whole, whole, tpeer(1)).wait_recv()

    def sent(name, whole):
        remote(name, whole, whole, tpeer(1)).wait_send()

    barrier = pltpu.get_barrier_semaphore()
    for r in range(1, 4):
        pl.semaphore_signal(barrier, 1, device_id=ypeer(r), device_id_type=MESH)
    for r in range(1, 4):
        pl.semaphore_signal(barrier, 1, device_id=zpeer(r), device_id_type=MESH)
    for r in range(1, 8):
        pl.semaphore_signal(barrier, 1, device_id=tpeer(r), device_id_type=MESH)

    loads = {}
    todo = [
        ("x", x_hbm, x_v), ("ag", ag_hbm, ag_v),
        ("wk", wk_hbm, qkv_v.at[1]), ("wv", wv_hbm, qkv_v.at[2]), ("wq", wq_hbm, qkv_v.at[0]),
        ("pk", pk_hbm, past.at[0, pl.ds(0, 128)]), ("pv", pv_hbm, pv_v),
        ("seg", seg_hbm, idall.at[0, 0]), ("creq", creq_hbm, idall.at[0, 1]),
        ("emb", emb_hbm, emb_v), ("wo", wo_hbm, wo_v), ("fg", fg_hbm, fg_v),
        ("wg", wg_hbm, ffn_v.at[0]), ("wu", wu_hbm, ffn_v.at[1]), ("wd", wd_hbm, ffn_v.at[2]),
        ("lg", lg_hbm, lg_v), ("lm", lm_hbm, lm_v),
    ]
    for i, (name, src, dst) in enumerate(todo):
        loads[name] = pltpu.make_async_copy(src, dst, lsem.at[i])
        loads[name].start()

    def gain_of(ref):
        return ref[...].astype(F32).reshape(1, 1024)

    loads["x"].wait()
    loads["ag"].wait()
    a_gain = gain_of(ag_v)
    normed = norm(x_v[...].astype(F32), a_gain)
    loads["wk"].wait()
    new[0, 0:128, :] = dot(normed, qkv_v[1]).astype(BF16)
    loads["wv"].wait()
    values = dot(normed, qkv_v[2])
    vrow[...] = values.astype(BF16)
    new[0, 128:256, :] = values.T.astype(BF16)
    loads["wq"].wait()
    queries = dot(normed, qkv_v[0]).astype(BF16).astype(F32) * 0.125
    qbuf[0] = queries.T.astype(BF16)
    loads["pk"].wait()
    loads["pv"].wait()
    past[0, 128:256, :] = pv_v[...].astype(F32).T.astype(BF16)
    loads["seg"].wait()
    loads["creq"].wait()

    pl.semaphore_wait(barrier, 13)

    for d in range(1, 4):
        remote("new", new.at[0], new.at[d], ypeer(d)).start()
    for e in range(1, 4):
        remote("q", qbuf.at[0], qbuf.at[e], zpeer(e)).start()
    for d in range(1, 4):
        remote("past", past.at[0], past.at[d], ypeer(d)).start()
    for d in range(1, 4):
        remote("ids", idall.at[0], idall.at[d], ypeer(d)).start()
        remote("ids", idall.at[0], idall.at[3 + d], zpeer(d)).start()

    first_row = (c * 8 + t) * 251
    row16 = lax.broadcasted_iota(jnp.int32, (16, 251), 0)
    col16 = lax.broadcasted_iota(jnp.int32, (16, 251), 1) + first_row
    wanted = jnp.full((16, 251), -1, jnp.int32)
    for q in range(4):
        wanted = jnp.where(row16 == q, ids_ref[q], wanted)
    one_hot = (col16 == wanted).astype(F32).astype(BF16)
    loads["emb"].wait()
    e1buf[0] = dot(one_hot, emb_v[...])[0:4].astype(BF16)
    for d in range(1, 4):
        remote("e1", e1buf.at[0], e1buf.at[d], ypeer(d)).start()

    my_columns = pl.ds(pl.multiple_of(t * 128, 128), 128)
    my_rows = pl.ds(pl.multiple_of(t * 16, 16), 16)

    def rows_of(r):
        return pl.ds(pl.multiple_of(lax.rem(t + r, 8) * 16, 16), 16)

    for r in range(1, 8):
        remote("relk", new.at[0, rows_of(r)], relk_ref.at[:, my_columns], tpeer(r)).start()
        remote("relv", vrow.at[rows_of(r)], relv_ref.at[:, my_columns], tpeer(r)).start()
    relk_ref[:, my_columns] = new[0, my_rows, :]
    relv_ref[:, my_columns] = vrow[my_rows, :]

    arrived("ids", idall.at[pl.ds(1, 6)])
    id_rows = [idall[d, 0:1, :].astype(F32) for d in range(4)]
    id_rows += [idall[d, 1:2, :].astype(F32) for d in range(4)]
    id_columns = jnp.concatenate(id_rows + [jnp.zeros((120, 128), F32)], axis=0).T
    for b in range(8):
        kid_s[b] = jnp.broadcast_to(id_columns[:, b : b + 1], (128, 128))
    idall[7] = idall[0]
    arrived("q", qbuf.at[pl.ds(1, 3)])
    arrived("new", new.at[pl.ds(1, 3)])
    arrived("past", past.at[pl.ds(1, 3)])

    def block(b):
        return new.at[b] if b < 4 else past.at[b - 4]

    arrived("e1", e1buf.at[pl.ds(1, 3)])
    e2buf[0] = sum(e1buf[d].astype(F32) for d in range(4)).astype(BF16)
    for e in range(1, 4):
        remote("e2", e2buf.at[0], e2buf.at[e], zpeer(e)).start()

    k_iota = lax.broadcasted_iota(jnp.int32, (128, 128), 0)
    q_iota = lax.broadcasted_iota(jnp.int32, (128, 128), 1)

    def attend(i, _):
        e = lax.rem(i + 1, 4)
        qt = qbuf[e]
        top = qt[0:64, :]
        low = qt[64:128, :]
        zero = jnp.zeros((64, 128), BF16)
        qd = jnp.concatenate(
            [jnp.concatenate([top, zero], axis=1), jnp.concatenate([zero, low], axis=1)], axis=0)
        qid = idall[4 + lax.rem(e + 3, 4), 0:1, :].astype(F32)
        q_at = y * 512 + lax.rem(zc - e + 4, 4) * 128
        highest = jnp.full((8, 256), FLOOR, F32)
        for b in range(8):
            s = dot(block(b)[0:128, :], qd)
            ok = kid_s[b] == qid
            if b < 4:
                k_at = lax.rem(y - b + 4, 4) * 512 + zc * 128
                ok = ok & (k_iota + (k_at - q_at) <= q_iota)
            s = jnp.where(jnp.concatenate([ok, ok], axis=1), s, NEG)
            s_s[b * 128 : (b + 1) * 128, :] = s
            highest = jnp.maximum(highest, jnp.max(s.reshape(16, 8, 256), axis=0))
        m = jnp.max(highest, axis=0, keepdims=True)
        total_w = jnp.zeros((8, 256), F32)
        o = jnp.zeros((128, 256), F32)
        for b in range(8):
            w = jnp.exp(s_s[b * 128 : (b + 1) * 128, :] - m)
            total_w = total_w + jnp.sum(w.reshape(16, 8, 256), axis=0)
            o = o + dot(block(b)[128:256, :], w.astype(BF16))
        l = jnp.sum(total_w, axis=0, keepdims=True)
        f = lax.rem(4 - e, 4)
        osend[f] = jnp.concatenate([o[0:64, 0:128], o[64:128, 128:256]], axis=0).astype(BF16)
        stsend[f] = jnp.concatenate(
            [m[:, 0:128], m[:, 128:256], l[:, 0:128], l[:, 128:256], jnp.zeros((4, 128), F32)],
            axis=0)

        @pl.when(i < 3)
        def _():
            remote("part", osend.at[f], obuf.at[f], zpeer(f)).start()
            remote("stats", stsend.at[f], stbuf.at[f], zpeer(f)).start()

        return 0

    lax.fori_loop(0, 4, attend, 0)
    obuf[0] = osend[0]
    stbuf[0] = stsend[0]

    arrived("e2", e2buf.at[pl.ds(1, 3)])
    e3buf[0] = sum(e2buf[e].astype(F32) for e in range(4)).astype(BF16)
    for r in range(1, 8):
        remote("e3", e3buf.at[0], e3buf.at[r], tpeer(r)).start()

    arrived("part", obuf.at[pl.ds(1, 3)])
    arrived("stats", stbuf.at[pl.ds(1, 3)])
    stats = [stbuf[f] for f in range(4)]
    tops = [st[0:2] for st in stats]
    joint = jnp.maximum(jnp.maximum(tops[0], tops[1]), jnp.maximum(tops[2], tops[3]))
    scales = [jnp.exp(m - joint) for m in tops]
    weight = sum(sc * st[2:4] for sc, st in zip(scales, stats))
    inverse = 1.0 / weight
    attended = jnp.zeros((128, 128), F32)
    for f in range(4):
        factor = scales[f] * inverse
        spread = jnp.concatenate(
            [jnp.broadcast_to(factor[0:1], (64, 128)), jnp.broadcast_to(factor[1:2], (64, 128))],
            axis=0)
        attended = attended + obuf[f].astype(F32) * spread
    loads["wo"].wait()
    head_term = dot(attended.T.astype(BF16), wo_v[...])
    part_s[0] = head_term.astype(BF16)
    for r in range(1, 8):
        remote("rs1", part_s.at[0, rows_of(r)], rs1buf.at[r], tpeer(r)).start()

    arrived("e3", e3buf.at[pl.ds(1, 7)])
    embedded = sum(e3buf[r].astype(F32) for r in range(8))

    def padded(rows):
        return jnp.concatenate([rows, jnp.zeros((12,) + rows.shape[1:], F32)], axis=0).astype(BF16)

    d_normed = padded(norm(embedded, a_gain).astype(F32))
    dq = dot(d_normed, qkv_v[0]).astype(BF16).astype(F32)[0:4] * 0.125
    dk = dot(d_normed, qkv_v[1]).astype(BF16).astype(F32)[0:4]
    dv = dot(d_normed, qkv_v[2]).astype(BF16).astype(F32)[0:4]
    lane4 = lax.broadcasted_iota(jnp.int32, (4, 128), 1)
    qd8 = jnp.concatenate(
        [jnp.where(lane4 < 64, dq, 0.0), jnp.where(lane4 >= 64, dq, 0.0)], axis=0)
    qd16 = jnp.concatenate([qd8, jnp.zeros((8, 128), F32)], axis=0).astype(BF16)
    k_ids = jnp.concatenate(id_rows, axis=1)
    rid = (lax.broadcasted_iota(jnp.int32, (16, 1024), 0) % 4).astype(F32)
    s = jnp.concatenate([dot_nt(qd16, block(b)[0:128, :]) for b in range(8)], axis=1)
    s = jnp.where(rid == k_ids, s, NEG)
    m = jnp.maximum(jnp.max(s, axis=1, keepdims=True), FLOOR)
    w = jnp.exp(s - m)
    l = jnp.sum(w, axis=1, keepdims=True)
    w = w.astype(BF16)
    o = sum(
        dot_nt(w[:, b * 128 : (b + 1) * 128], block(b)[128:256, :]) for b in range(8))
    dbuf[0, 0:8, :] = o[0:8]
    dbuf[0, 8:16, :] = jnp.broadcast_to(m[0:8], (8, 128))
    dbuf[0, 16:24, :] = jnp.broadcast_to(l[0:8], (8, 128))
    for e in range(1, 4):
        remote("dpart", dbuf.at[0], dbuf.at[e], zpeer(e)).start()

    residual = x_v[my_rows, :].astype(F32) + part_s[0, my_rows, :].astype(F32)
    arrived("rs1", rs1buf.at[pl.ds(1, 7)])
    for r in range(1, 8):
        residual = residual + rs1buf[r].astype(F32)
    loads["fg"].wait()
    f_gain = gain_of(fg_v)
    nbuf[my_rows, :] = norm(residual, f_gain)
    for r in range(1, 8):
        remote("ag1", nbuf.at[my_rows], nbuf.at[my_rows], tpeer(r)).start()
    fin_s[...] = residual

    own_m = jnp.sum(qd8 * jnp.concatenate([dk, dk], axis=0), axis=1, keepdims=True)
    own_m = jnp.broadcast_to(own_m, (8, 128))
    arrived("dpart", dbuf.at[pl.ds(1, 3)])
    dparts = [dbuf[e] for e in range(4)]
    joint = own_m
    for part in dparts:
        joint = jnp.maximum(joint, part[8:16])
    own_scale = jnp.exp(own_m - joint)
    weight = own_scale
    summed = own_scale * jnp.concatenate([dv, dv], axis=0)
    for part in dparts:
        scale = jnp.exp(part[8:16] - joint)
        weight = weight + scale * part[16:24]
        summed = summed + scale * part[0:8]
    summed = summed / weight
    d_attended = padded(jnp.where(lane4 < 64, summed[0:4], summed[4:8]))
    ar1buf[0] = dot(d_attended, wo_v[...])[0:4].astype(BF16)
    for r in range(1, 8):
        remote("ar1", ar1buf.at[0], ar1buf.at[r], tpeer(r)).start()

    def units(rows):
        gate = dot_nt(rows, ffn_v[0])
        up = dot_nt(rows, ffn_v[1])
        hidden = (jax.nn.gelu(gate, approximate=True) * up).astype(BF16)
        return dot(hidden, ffn_v[2])

    loads["wg"].wait()
    loads["wu"].wait()
    loads["wd"].wait()
    arrived("ag1", nbuf.at[pl.ds(0, 112)])
    part_s[1] = units(nbuf[...]).astype(BF16)
    for r in range(1, 8):
        remote("rs2", part_s.at[1, rows_of(r)], rs2buf.at[r], tpeer(r)).start()

    arrived("ar1", ar1buf.at[pl.ds(1, 7)])
    d_residual = embedded + sum(ar1buf[r].astype(F32) for r in range(8))
    ar2buf[0] = units(padded(norm(d_residual, f_gain).astype(F32)))[0:4].astype(BF16)
    for r in range(1, 8):
        remote("ar2", ar2buf.at[0], ar2buf.at[r], tpeer(r)).start()

    final = fin_s[...] + part_s[1, my_rows, :].astype(F32)
    arrived("rs2", rs2buf.at[pl.ds(1, 7)])
    for r in range(1, 8):
        final = final + rs2buf[r].astype(F32)
    out_ref[my_rows, :] = final.astype(BF16)
    for r in range(1, 8):
        remote("ag2", out_ref.at[my_rows], out_ref.at[my_rows], tpeer(r)).start()

    arrived("ar2", ar2buf.at[pl.ds(1, 7)])
    d_final = d_residual + sum(ar2buf[r].astype(F32) for r in range(8))
    loads["lg"].wait()
    loads["lm"].wait()
    l_normed = padded(norm(d_final, gain_of(lg_v)).astype(F32))
    logits_ref[...] = dot(l_normed, lm_v[...])[0:4]

    arrived("relk", relk_ref.at[:, pl.ds(0, 896)])
    arrived("relv", relv_ref.at[:, pl.ds(0, 896)])
    sent("new", new.at[pl.ds(1, 3)])
    sent("past", past.at[pl.ds(1, 3)])
    sent("ids", idall.at[pl.ds(1, 6)])
    sent("q", qbuf.at[pl.ds(1, 3)])
    sent("e1", e1buf.at[pl.ds(1, 3)])
    sent("e2", e2buf.at[pl.ds(1, 3)])
    sent("e3", e3buf.at[pl.ds(1, 7)])
    sent("relk", relk_ref.at[:, pl.ds(0, 896)])
    sent("relv", relv_ref.at[:, pl.ds(0, 896)])
    sent("part", obuf.at[pl.ds(1, 3)])
    sent("stats", stbuf.at[pl.ds(1, 3)])
    sent("dpart", dbuf.at[pl.ds(1, 3)])
    sent("rs1", rs1buf.at[pl.ds(1, 7)])
    sent("ar1", ar1buf.at[pl.ds(1, 7)])
    sent("ag1", nbuf.at[pl.ds(0, 112)])
    sent("rs2", rs2buf.at[pl.ds(1, 7)])
    sent("ar2", ar2buf.at[pl.ds(1, 7)])
    arrived("ag2", out_ref.at[pl.ds(0, 112)])
    sent("ag2", out_ref.at[pl.ds(0, 112)])


def hand_over(*refs):
    sems = refs[8]
    copies = [pltpu.make_async_copy(refs[i], refs[4 + i], sems.at[i]) for i in range(4)]
    for copy in copies:
        copy.start()
    for copy in copies:
        copy.wait()


def on_device(
    prompt_states, segment_ids, past_keys, past_values, cache_request, decode_ids, embed_table,
    attn_gain, ff_gain, final_gain, w_query, w_key, w_value, w_out, w_gate, w_up, w_down, lm_head,
):
    in_hbm = pl.BlockSpec(memory_space=pltpu.HBM)
    in_vmem = pl.BlockSpec(memory_space=pltpu.VMEM)
    dma = pltpu.SemaphoreType.DMA
    local = [
        ((128, 1024), BF16), ((1024,), BF16), ((1024,), BF16), ((1024,), BF16),
        ((3, 1024, 128), BF16), ((128, 1024), BF16), ((3, 352, 1024), BF16), ((1024, 251), BF16),
        ((251, 1024), BF16), ((128, 128), BF16),
        ((128, 128), BF16), ((8, 128, 128), F32), ((1024, 256), F32), ((8, 128), BF16),
        ((4, 128, 128), BF16), ((4, 8, 128), F32), ((2, 128, 1024), BF16), ((128, 1024), BF16),
        ((8, 128), BF16), ((16, 1024), F32),
    ]
    arriving = [
        ((4, 256, 128), BF16), ((4, 256, 128), BF16), ((8, 8, 128), jnp.int32),
        ((4, 128, 128), BF16), ((4, 128, 128), BF16), ((4, 8, 128), F32), ((4, 24, 128), F32),
        ((4, 4, 1024), BF16), ((4, 4, 1024), BF16), ((8, 4, 1024), BF16),
        ((8, 16, 1024), BF16), ((8, 4, 1024), BF16), ((8, 16, 1024), BF16), ((8, 4, 1024), BF16),
    ]
    shapes = [((128, 1024), BF16), ((4, 251), F32), ((16, 1024), BF16), ((16, 1024), BF16)]
    arrays = [
        pltpu.with_memory_space_constraint(a, pltpu.HBM)
        for a in (
            prompt_states, segment_ids, past_keys, past_values, cache_request, embed_table,
            attn_gain, ff_gain, final_gain, w_query, w_key, w_value, w_out, w_gate.T, w_up.T,
            w_down, lm_head,
        )
    ]
    results = pl.pallas_call(
        kernel,
        out_shape=tuple(pltpu.VMEM(s, d) for s, d in shapes),
        in_specs=[pl.BlockSpec(memory_space=pltpu.SMEM)] + [in_hbm] * 17,
        out_specs=(in_vmem,) * 4,
        scratch_shapes=[pltpu.VMEM(s, d) for s, d in local + arriving]
        + [dma((17,)), dma((18,)), dma((18,))],
        compiler_params=pltpu.CompilerParams(
            collective_id=0, has_side_effects=True, vmem_limit_bytes=60 * 1024 * 1024),
    )(decode_ids, *arrays)
    results = [pltpu.with_memory_space_constraint(a, pltpu.VMEM) for a in results]
    return pl.pallas_call(
        hand_over,
        out_shape=tuple(jax.ShapeDtypeStruct(s, d) for s, d in shapes),
        in_specs=[in_vmem] * 4,
        out_specs=(in_hbm,) * 4,
        scratch_shapes=[dma((4,))],
    )(*results)


def solution(mesh):
    placed = (
        P("ctx", None),
        P("ctx"),
        P("ctx", "tp"),
        P("ctx", "tp"),
        P("ctx"),
        P(),
        P(("ctx", "tp"), None),
        P(),
        P(),
        P(),
        P(None, "tp"),
        P(None, "tp"),
        P(None, "tp"),
        P("tp", None),
        P(None, "tp"),
        P(None, "tp"),
        P("tp", None),
        P(None, ("ctx", "tp")),
    )
    return jax.shard_map(
        on_device,
        mesh=mesh,
        in_specs=placed,
        out_specs=(
            P("ctx", None),
            P(None, ("ctx", "tp")),
            P(("ctx", "tp"), None),
            P(("ctx", "tp"), None),
        ),
        check_vma=False,
    )
```

```python
import jax
import jax.numpy as jnp
from jax import lax
from jax.experimental import pallas as pl
from jax.experimental.pallas import tpu as pltpu
from jax.sharding import PartitionSpec as P

DH = 64
EPS = 1e-06
NEG = -1e30
FLOOR = -1e29
MESH = pl.DeviceIdType.MESH
F32 = jnp.float32
BF16 = jnp.bfloat16


def dot(a, b):
    return jnp.dot(a, b, preferred_element_type=F32)


def dot_nt(a, b):
    return lax.dot_general(a, b, (((1,), (1,)), ((), ())), preferred_element_type=F32)


def norm(states, gain):
    mean_square = jnp.mean(states * states, axis=-1, keepdims=True)
    return (states * lax.rsqrt(mean_square + EPS) * gain).astype(BF16)


def kernel(
    ids_ref, x_hbm, seg_hbm, pk_hbm, pv_hbm, creq_hbm, emb_hbm,
    ag_hbm, fg_hbm, lg_hbm, wq_hbm, wk_hbm, wv_hbm, wo_hbm, wg_hbm, wu_hbm, wd_hbm, lm_hbm,
    out_ref, logits_ref, relk_ref, relv_ref,
    x_v, ag_v, fg_v, lg_v, qkv_v, ffn_v, lm_v, emb_v, pv_v,
    vrow, kid_s, s_s, hi_s, tw_s, o_s, osend, stsend, part_s, nbuf, res_s,
    past, new, idall, qbuf, obuf, stbuf, dbuf, e1buf, e2buf, e3buf,
    wo_full, abuf, dabuf, rs2buf, ar2buf,
    lsem, ssem, rsem,
):
    c = lax.axis_index("ctx")
    t = lax.axis_index("tp")
    y = lax.div(c, 4)
    zc = lax.rem(c, 4)
    z_hi = lax.div(zc, 2)
    core = lax.rem(c, 2)
    z_lo = lax.div(t, 4)
    x = lax.rem(t, 4)

    def ypeer(d):
        return (lax.rem(y + d, 4) * 4 + zc, t)

    def zc_of(g):
        return lax.rem(z_hi + lax.div(g, 2), 2) * 2 + lax.rem(core + lax.rem(g, 2), 2)

    def zpeer(g):
        return (y * 4 + zc_of(jnp.int32(g)), t)

    def t_of(r):
        return lax.rem(z_lo + r // 4, 2) * 4 + lax.rem(x + r % 4, 4)

    def tpeer(r):
        return (c, t_of(r))

    y_order = (2, 1, 3)
    z_order = (3, 2, 1)
    t_order = (6, 5, 7, 2, 4, 1, 3)

    names = (
        "past", "new1", "new2", "new3", "ids", "q", "e1", "e2", "e3", "relk", "relv",
        "part", "stats", "dpart", "wo", "woz", "wof", "swap", "att", "datt", "rs2", "ar2", "ag2",
    )

    def remote(name, src, dst, peer):
        at = names.index(name)
        return pltpu.make_async_remote_copy(
            src_ref=src, dst_ref=dst, send_sem=ssem.at[at], recv_sem=rsem.at[at],
            device_id=peer, device_id_type=MESH,
        )

    def arrived(name, whole):
        remote(name, whole, whole, tpeer(1)).wait_recv()

    def sent(name, whole):
        remote(name, whole, whole, tpeer(1)).wait_send()

    barrier = pltpu.get_barrier_semaphore()
    for r in range(1, 4):
        pl.semaphore_signal(barrier, 1, device_id=ypeer(r), device_id_type=MESH)
    for r in range(1, 4):
        pl.semaphore_signal(barrier, 1, device_id=zpeer(r), device_id_type=MESH)
    for r in range(1, 8):
        pl.semaphore_signal(barrier, 1, device_id=tpeer(r), device_id_type=MESH)

    my_half = pl.ds(pl.multiple_of(core * 64, 64), 64)
    loads = {}
    todo = [
        ("x", x_hbm, x_v), ("ag", ag_hbm, ag_v),
        ("wk", wk_hbm, qkv_v.at[1]), ("wv", wv_hbm, qkv_v.at[2]), ("wq", wq_hbm, qkv_v.at[0]),
        ("pk", pk_hbm, past.at[0, pl.ds(0, 128)]), ("pv", pv_hbm, pv_v),
        ("seg", seg_hbm, idall.at[0, 0]), ("creq", creq_hbm, idall.at[0, 1]),
        ("emb", emb_hbm, emb_v), ("wo", wo_hbm.at[my_half], wo_full.at[t, core]), ("fg", fg_hbm, fg_v),
        ("wg", wg_hbm, ffn_v.at[0]), ("wu", wu_hbm, ffn_v.at[1]), ("wd", wd_hbm, ffn_v.at[2]),
        ("lg", lg_hbm, lg_v), ("lm", lm_hbm, lm_v),
    ]
    for i, (name, src, dst) in enumerate(todo):
        loads[name] = pltpu.make_async_copy(src, dst, lsem.at[i])
        loads[name].start()

    def gain_of(ref):
        return ref[...].astype(F32).reshape(1, 1024)

    loads["x"].wait()
    loads["ag"].wait()
    a_gain = gain_of(ag_v)
    normed = norm(x_v[...].astype(F32), a_gain)
    loads["wk"].wait()
    new[0, 0:128, :] = dot(normed, qkv_v[1]).astype(BF16)
    loads["wv"].wait()
    values = dot(normed, qkv_v[2])
    vrow[...] = values.astype(BF16)
    new[0, 128:256, :] = values.T.astype(BF16)
    loads["wq"].wait()
    queries = dot(normed, qkv_v[0]).astype(BF16).astype(F32) * 0.125
    qbuf[0] = queries.T.astype(BF16)
    loads["pk"].wait()
    loads["pv"].wait()
    past[0, 128:256, :] = pv_v[...].astype(F32).T.astype(BF16)
    loads["seg"].wait()
    loads["creq"].wait()

    pl.semaphore_wait(barrier, 13)

    def send_new(d):
        remote("new%d" % d, new.at[0], new.at[d], ypeer(d)).start()

    for d in (2, 1):
        pl.when(y + d < 4)(lambda d=d: send_new(d))
    for g in z_order:
        remote("q", qbuf.at[0], qbuf.at[g], zpeer(g)).start()
    for d in y_order:
        remote("past", past.at[0], past.at[d], ypeer(d)).start()
    for d in y_order:
        remote("ids", idall.at[0], idall.at[d], ypeer(d)).start()
    for g in z_order:
        remote("ids", idall.at[0], idall.at[3 + g], zpeer(g)).start()

    first_row = (c * 8 + t) * 251
    row16 = lax.broadcasted_iota(jnp.int32, (16, 251), 0)
    col16 = lax.broadcasted_iota(jnp.int32, (16, 251), 1) + first_row
    wanted = jnp.full((16, 251), -1, jnp.int32)
    for q in range(4):
        wanted = jnp.where(row16 == q, ids_ref[q], wanted)
    one_hot = (col16 == wanted).astype(F32).astype(BF16)
    loads["emb"].wait()
    e1buf[0] = dot(one_hot, emb_v[...])[0:4].astype(BF16)
    for r in t_order:
        remote("e1", e1buf.at[0], e1buf.at[r], tpeer(r)).start()

    remote("woz", wo_hbm.at[my_half], wo_full.at[t, core], tpeer(4)).start()
    for r in (2, 1, 3):
        remote("wo", wo_hbm.at[my_half], wo_full.at[t, core], tpeer(r)).start()

    my_columns = pl.ds(pl.multiple_of(t * 128, 128), 128)
    my_rows = pl.ds(pl.multiple_of(t * 16, 16), 16)

    def rows_of(r):
        return pl.ds(pl.multiple_of(t_of(r) * 16, 16), 16)

    for d in (2, 1):
        pl.when(y + d >= 4)(lambda d=d: send_new(d))
    send_new(3)
    for r in t_order:
        remote("relk", new.at[0, rows_of(r)], relk_ref.at[:, my_columns], tpeer(r)).start()
        remote("relv", vrow.at[rows_of(r)], relv_ref.at[:, my_columns], tpeer(r)).start()
    relk_ref[:, my_columns] = new[0, my_rows, :]
    relv_ref[:, my_columns] = vrow[my_rows, :]

    arrived("woz", wo_full.at[0, 0])
    across = t_of(4)
    for r in (2, 1, 3):
        remote("wof", wo_full.at[across, core], wo_full.at[across, core], tpeer(r)).start()

    arrived("e1", e1buf.at[pl.ds(1, 7)])
    e2buf[0] = sum(e1buf[r].astype(F32) for r in range(8)).astype(BF16)
    for g in z_order:
        remote("e2", e2buf.at[0], e2buf.at[g], zpeer(g)).start()

    arrived("ids", idall.at[pl.ds(1, 6)])
    new_ids = [idall[d, 0:1, :].astype(F32) for d in range(4)]
    past_ids = [idall[d, 1:2, :].astype(F32) for d in range(4)]
    id_columns = jnp.concatenate(
        new_ids + past_ids + [jnp.zeros((120, 128), F32)], axis=0).T
    for b in range(8):
        kid_s[b] = jnp.broadcast_to(id_columns[:, b : b + 1], (128, 128))
    idall[7] = idall[0]
    arrived("q", qbuf.at[pl.ds(1, 3)])
    pl.when(y >= 1)(lambda: arrived("new1", new.at[1]))
    pl.when(y >= 2)(lambda: arrived("new2", new.at[2]))
    arrived("past", past.at[pl.ds(1, 3)])

    def block(b):
        return new.at[b] if b < 4 else past.at[b - 4]

    k_iota = lax.broadcasted_iota(jnp.int32, (128, 128), 0)
    q_iota = lax.broadcasted_iota(jnp.int32, (128, 128), 1)

    def attend(i, _):
        g = 3 - i
        qt = qbuf[g]
        top = qt[0:64, :]
        low = qt[64:128, :]
        zero = jnp.zeros((64, 128), BF16)
        qd = jnp.concatenate(
            [jnp.concatenate([top, zero], axis=1), jnp.concatenate([zero, low], axis=1)], axis=0)
        qid = idall[4 + lax.rem(g + 3, 4), 0:1, :].astype(F32)
        q_at = y * 512 + zc_of(g) * 128

        def score(b):
            s = dot(block(b)[0:128, :], qd)
            ok = kid_s[b] == qid
            if b < 4:
                k_at = (y - b) * 512 + zc * 128
                ok = ok & (k_iota + (k_at - q_at) <= q_iota)
            s = jnp.where(jnp.concatenate([ok, ok], axis=1), s, NEG)
            s_s[b * 128 : (b + 1) * 128, :] = s
            return jnp.max(s.reshape(16, 8, 256), axis=0)

        def weigh(b, m):
            w = jnp.exp(s_s[b * 128 : (b + 1) * 128, :] - m)
            return jnp.sum(w.reshape(16, 8, 256), axis=0), dot(
                block(b)[128:256, :], w.astype(BF16))

        always = (0, 4, 5, 6, 7)
        highest = jnp.full((8, 256), FLOOR, F32)
        for b in always:
            highest = jnp.maximum(highest, score(b))
        hi_s[...] = highest

        def score_more(b):
            hi_s[...] = jnp.maximum(hi_s[...], score(b))

        pl.when(y >= 1)(lambda: score_more(1))
        pl.when(y >= 2)(lambda: score_more(2))
        m = jnp.max(hi_s[...], axis=0, keepdims=True)
        total_w = jnp.zeros((8, 256), F32)
        o = jnp.zeros((128, 256), F32)
        for b in always:
            more_w, more_o = weigh(b, m)
            total_w = total_w + more_w
            o = o + more_o
        tw_s[...] = total_w
        o_s[...] = o

        def weigh_more(b):
            more_w, more_o = weigh(b, m)
            tw_s[...] += more_w
            o_s[...] += more_o

        pl.when(y >= 1)(lambda: weigh_more(1))
        pl.when(y >= 2)(lambda: weigh_more(2))
        l = jnp.sum(tw_s[...], axis=0, keepdims=True)
        osend[g] = jnp.concatenate(
            [o_s[0:64, 0:128], o_s[64:128, 128:256]], axis=0).astype(BF16)
        stsend[g] = jnp.concatenate(
            [m[:, 0:128], m[:, 128:256], l[:, 0:128], l[:, 128:256], jnp.zeros((4, 128), F32)],
            axis=0)

        @pl.when(i < 3)
        def _():
            remote("part", osend.at[g], obuf.at[g], zpeer(g)).start()
            remote("stats", stsend.at[g], stbuf.at[g], zpeer(g)).start()

        return 0

    lax.fori_loop(0, 4, attend, 0)
    obuf[0] = osend[0]
    stbuf[0] = stsend[0]

    arrived("e2", e2buf.at[pl.ds(1, 3)])
    e3buf[0] = sum(e2buf[g].astype(F32) for g in range(4)).astype(BF16)
    for d in y_order:
        remote("e3", e3buf.at[0], e3buf.at[d], ypeer(d)).start()

    arrived("part", obuf.at[pl.ds(1, 3)])
    arrived("stats", stbuf.at[pl.ds(1, 3)])
    stats = [stbuf[f] for f in range(4)]
    tops = [st[0:2] for st in stats]
    joint = jnp.maximum(jnp.maximum(tops[0], tops[1]), jnp.maximum(tops[2], tops[3]))
    scales = [jnp.exp(m - joint) for m in tops]
    weight = sum(sc * st[2:4] for sc, st in zip(scales, stats))
    inverse = 1.0 / weight
    attended = jnp.zeros((128, 128), F32)
    for f in range(4):
        factor = scales[f] * inverse
        spread = jnp.concatenate(
            [jnp.broadcast_to(factor[0:1], (64, 128)), jnp.broadcast_to(factor[1:2], (64, 128))],
            axis=0)
        attended = attended + obuf[f].astype(F32) * spread
    abuf[:, my_columns] = attended.T.astype(BF16)
    for r in t_order:
        remote("att", abuf.at[:, my_columns], abuf.at[:, my_columns], tpeer(r)).start()

    arrived("wo", wo_full.at[pl.ds(0, 3), 0])
    arrived("wof", wo_full.at[pl.ds(0, 3), 0])
    loads["wo"].wait()
    remote("swap", wo_full.at[:, core], wo_full.at[:, core], zpeer(1)).start()

    arrived("e3", e3buf.at[pl.ds(1, 3)])
    embedded = sum(e3buf[d].astype(F32) for d in range(4))
    pl.when(y < 1)(lambda: arrived("new1", new.at[1]))
    pl.when(y < 2)(lambda: arrived("new2", new.at[2]))
    arrived("new3", new.at[3])

    def padded(rows):
        return jnp.concatenate([rows, jnp.zeros((12,) + rows.shape[1:], F32)], axis=0).astype(BF16)

    d_normed = padded(norm(embedded, a_gain).astype(F32))
    dq = dot(d_normed, qkv_v[0]).astype(BF16).astype(F32)[0:4] * 0.125
    dk = dot(d_normed, qkv_v[1]).astype(BF16).astype(F32)[0:4]
    dv = dot(d_normed, qkv_v[2]).astype(BF16).astype(F32)[0:4]
    lane4 = lax.broadcasted_iota(jnp.int32, (4, 128), 1)
    qd8 = jnp.concatenate(
        [jnp.where(lane4 < 64, dq, 0.0), jnp.where(lane4 >= 64, dq, 0.0)], axis=0)
    qd16 = jnp.concatenate([qd8, jnp.zeros((8, 128), F32)], axis=0).astype(BF16)
    k_ids = jnp.concatenate(new_ids + past_ids, axis=1)
    rid = (lax.broadcasted_iota(jnp.int32, (16, 1024), 0) % 4).astype(F32)
    s = jnp.concatenate([dot_nt(qd16, block(b)[0:128, :]) for b in range(8)], axis=1)
    s = jnp.where(rid == k_ids, s, NEG)
    m = jnp.maximum(jnp.max(s, axis=1, keepdims=True), FLOOR)
    w = jnp.exp(s - m)
    l = jnp.sum(w, axis=1, keepdims=True)
    w = w.astype(BF16)
    o = sum(
        dot_nt(w[:, b * 128 : (b + 1) * 128], block(b)[128:256, :]) for b in range(8))
    dbuf[0, 0:8, :] = o[0:8]
    dbuf[0, 8:16, :] = jnp.broadcast_to(m[0:8], (8, 128))
    dbuf[0, 16:24, :] = jnp.broadcast_to(l[0:8], (8, 128))
    for g in z_order:
        remote("dpart", dbuf.at[0], dbuf.at[g], zpeer(g)).start()

    own_m = jnp.sum(qd8 * jnp.concatenate([dk, dk], axis=0), axis=1, keepdims=True)
    own_m = jnp.broadcast_to(own_m, (8, 128))
    arrived("dpart", dbuf.at[pl.ds(1, 3)])
    dparts = [dbuf[e] for e in range(4)]
    joint = own_m
    for part in dparts:
        joint = jnp.maximum(joint, part[8:16])
    own_scale = jnp.exp(own_m - joint)
    weight = own_scale
    summed = own_scale * jnp.concatenate([dv, dv], axis=0)
    for part in dparts:
        scale = jnp.exp(part[8:16] - joint)
        weight = weight + scale * part[16:24]
        summed = summed + scale * part[0:8]
    summed = summed / weight
    d_attended = jnp.where(lane4 < 64, summed[0:4], summed[4:8])
    dabuf[t] = d_attended.astype(BF16)
    for r in t_order:
        remote("datt", dabuf.at[t], dabuf.at[t], tpeer(r)).start()

    def units(rows):
        gate = dot_nt(rows, ffn_v[0])
        up = dot_nt(rows, ffn_v[1])
        hidden = (jax.nn.gelu(gate, approximate=True) * up).astype(BF16)
        return dot(hidden, ffn_v[2])

    arrived("swap", wo_full.at[:, 0])
    arrived("att", abuf.at[:, pl.ds(0, 896)])
    residual = x_v[...].astype(F32) + dot(abuf[...], wo_full[...].reshape(1024, 1024))
    res_s[...] = residual
    loads["fg"].wait()
    f_gain = gain_of(fg_v)
    nbuf[...] = norm(residual, f_gain)
    loads["wg"].wait()
    loads["wu"].wait()
    loads["wd"].wait()
    part_s[...] = units(nbuf[...]).astype(BF16)
    for r in t_order:
        remote("rs2", part_s.at[rows_of(r)], rs2buf.at[r], tpeer(r)).start()

    arrived("datt", dabuf.at[pl.ds(0, 7)])
    d_all = jnp.concatenate([dabuf[i].astype(F32) for i in range(8)], axis=1)
    d_residual = embedded + dot(padded(d_all), wo_full[...].reshape(1024, 1024))[0:4]
    ar2buf[0] = units(padded(norm(d_residual, f_gain).astype(F32)))[0:4].astype(BF16)
    for r in t_order:
        remote("ar2", ar2buf.at[0], ar2buf.at[r], tpeer(r)).start()

    final = res_s[my_rows, :] + part_s[my_rows, :].astype(F32)
    arrived("rs2", rs2buf.at[pl.ds(1, 7)])
    for r in range(1, 8):
        final = final + rs2buf[r].astype(F32)
    out_ref[my_rows, :] = final.astype(BF16)
    for r in t_order:
        remote("ag2", out_ref.at[my_rows], out_ref.at[my_rows], tpeer(r)).start()

    arrived("ar2", ar2buf.at[pl.ds(1, 7)])
    d_final = d_residual + sum(ar2buf[r].astype(F32) for r in range(8))
    loads["lg"].wait()
    loads["lm"].wait()
    l_normed = padded(norm(d_final, gain_of(lg_v)).astype(F32))
    logits_ref[...] = dot(l_normed, lm_v[...])[0:4]

    arrived("relk", relk_ref.at[:, pl.ds(0, 896)])
    arrived("relv", relv_ref.at[:, pl.ds(0, 896)])
    for d in range(1, 4):
        sent("new%d" % d, new.at[d])
    sent("past", past.at[pl.ds(1, 3)])
    sent("ids", idall.at[pl.ds(1, 6)])
    sent("q", qbuf.at[pl.ds(1, 3)])
    sent("e1", e1buf.at[pl.ds(1, 7)])
    sent("e2", e2buf.at[pl.ds(1, 3)])
    sent("e3", e3buf.at[pl.ds(1, 3)])
    sent("relk", relk_ref.at[:, pl.ds(0, 896)])
    sent("relv", relv_ref.at[:, pl.ds(0, 896)])
    sent("part", obuf.at[pl.ds(1, 3)])
    sent("stats", stbuf.at[pl.ds(1, 3)])
    sent("dpart", dbuf.at[pl.ds(1, 3)])
    sent("wo", wo_full.at[pl.ds(0, 3), 0])
    sent("woz", wo_full.at[0, 0])
    sent("wof", wo_full.at[pl.ds(0, 3), 0])
    sent("swap", wo_full.at[:, 0])
    sent("att", abuf.at[:, pl.ds(0, 896)])
    sent("datt", dabuf.at[pl.ds(0, 7)])
    sent("rs2", rs2buf.at[pl.ds(1, 7)])
    sent("ar2", ar2buf.at[pl.ds(1, 7)])
    arrived("ag2", out_ref.at[pl.ds(0, 112)])
    sent("ag2", out_ref.at[pl.ds(0, 112)])


def hand_over(*refs):
    sems = refs[8]
    copies = [pltpu.make_async_copy(refs[i], refs[4 + i], sems.at[i]) for i in range(4)]
    for copy in copies:
        copy.start()
    for copy in copies:
        copy.wait()


def on_device(
    prompt_states, segment_ids, past_keys, past_values, cache_request, decode_ids, embed_table,
    attn_gain, ff_gain, final_gain, w_query, w_key, w_value, w_out, w_gate, w_up, w_down, lm_head,
):
    in_hbm = pl.BlockSpec(memory_space=pltpu.HBM)
    in_vmem = pl.BlockSpec(memory_space=pltpu.VMEM)
    dma = pltpu.SemaphoreType.DMA
    local = [
        ((128, 1024), BF16), ((1024,), BF16), ((1024,), BF16), ((1024,), BF16),
        ((3, 1024, 128), BF16), ((3, 352, 1024), BF16), ((1024, 251), BF16),
        ((251, 1024), BF16), ((128, 128), BF16),
        ((128, 128), BF16), ((8, 128, 128), F32), ((1024, 256), F32), ((8, 256), F32),
        ((8, 256), F32), ((128, 256), F32), ((4, 128, 128), BF16), ((4, 8, 128), F32),
        ((128, 1024), BF16), ((128, 1024), BF16), ((128, 1024), F32),
    ]
    arriving = [
        ((4, 256, 128), BF16), ((4, 256, 128), BF16), ((8, 8, 128), jnp.int32),
        ((4, 128, 128), BF16), ((4, 128, 128), BF16), ((4, 8, 128), F32), ((4, 24, 128), F32),
        ((8, 4, 1024), BF16), ((4, 4, 1024), BF16), ((4, 4, 1024), BF16),
        ((8, 2, 64, 1024), BF16), ((128, 1024), BF16), ((8, 4, 128), BF16),
        ((8, 16, 1024), BF16), ((8, 4, 1024), BF16),
    ]
    shapes = [((128, 1024), BF16), ((4, 251), F32), ((16, 1024), BF16), ((16, 1024), BF16)]
    arrays = [
        pltpu.with_memory_space_constraint(a, pltpu.HBM)
        for a in (
            prompt_states, segment_ids, past_keys, past_values, cache_request, embed_table,
            attn_gain, ff_gain, final_gain, w_query, w_key, w_value, w_out, w_gate.T, w_up.T,
            w_down, lm_head,
        )
    ]
    results = pl.pallas_call(
        kernel,
        out_shape=tuple(pltpu.VMEM(s, d) for s, d in shapes),
        in_specs=[pl.BlockSpec(memory_space=pltpu.SMEM)] + [in_hbm] * 17,
        out_specs=(in_vmem,) * 4,
        scratch_shapes=[pltpu.VMEM(s, d) for s, d in local + arriving]
        + [dma((17,)), dma((23,)), dma((23,))],
        compiler_params=pltpu.CompilerParams(
            collective_id=0, has_side_effects=True, vmem_limit_bytes=60 * 1024 * 1024),
    )(decode_ids, *arrays)
    results = [pltpu.with_memory_space_constraint(a, pltpu.VMEM) for a in results]
    return pl.pallas_call(
        hand_over,
        out_shape=tuple(jax.ShapeDtypeStruct(s, d) for s, d in shapes),
        in_specs=[in_vmem] * 4,
        out_specs=(in_hbm,) * 4,
        scratch_shapes=[dma((4,))],
    )(*results)


def solution(mesh):
    placed = (
        P("ctx", None),
        P("ctx"),
        P("ctx", "tp"),
        P("ctx", "tp"),
        P("ctx"),
        P(),
        P(("ctx", "tp"), None),
        P(),
        P(),
        P(),
        P(None, "tp"),
        P(None, "tp"),
        P(None, "tp"),
        P("tp", None),
        P(None, "tp"),
        P(None, "tp"),
        P("tp", None),
        P(None, ("ctx", "tp")),
    )
    return jax.shard_map(
        on_device,
        mesh=mesh,
        in_specs=placed,
        out_specs=(
            P("ctx", None),
            P(None, ("ctx", "tp")),
            P(("ctx", "tp"), None),
            P(("ctx", "tp"), None),
        ),
        check_vma=False,
    )
```

```python
import jax
import jax.numpy as jnp
from jax import lax
from jax.experimental import pallas as pl
from jax.experimental.pallas import tpu as pltpu
from jax.sharding import PartitionSpec as P

DH = 64
EPS = 1e-06
NEG = -1e30
FLOOR = -1e29
MESH = pl.DeviceIdType.MESH
F32 = jnp.float32
BF16 = jnp.bfloat16


def dot(a, b):
    return jnp.dot(a, b, preferred_element_type=F32)


def dot_nt(a, b):
    return lax.dot_general(a, b, (((1,), (1,)), ((), ())), preferred_element_type=F32)


def norm(states, gain):
    mean_square = jnp.mean(states * states, axis=-1, keepdims=True)
    return (states * lax.rsqrt(mean_square + EPS) * gain).astype(BF16)


def kernel(
    ids_ref, x_hbm, seg_hbm, pk_hbm, pv_hbm, creq_hbm, emb_hbm,
    ag_hbm, fg_hbm, lg_hbm, wq_hbm, wk_hbm, wv_hbm, wo_hbm, wg_hbm, wu_hbm, wd_hbm, lm_hbm,
    out_ref, logits_ref, relk_ref, relv_ref,
    x_v, ag_v, fg_v, lg_v, qkv_v, ffn_v, lm_v, emb_v, pv_v,
    vrow, kid_s, s_s, hi_s, tw_s, o_s, osend, stsend, part_s, nbuf, res_s,
    past, new, idall, qbuf, obuf, stbuf, dbuf, e1buf, e2buf, e3buf,
    wo_full, abuf, dabuf, rs2buf, ar2buf,
    lsem, ssem, rsem,
):
    c = lax.axis_index("ctx")
    t = lax.axis_index("tp")
    y = lax.div(c, 4)
    zc = lax.rem(c, 4)
    z_hi = lax.div(zc, 2)
    core = lax.rem(c, 2)
    z_lo = lax.div(t, 4)
    x = lax.rem(t, 4)

    def ypeer(d):
        return (lax.rem(y + d, 4) * 4 + zc, t)

    def zc_of(g):
        return lax.rem(z_hi + lax.div(g, 2), 2) * 2 + lax.rem(core + lax.rem(g, 2), 2)

    def zpeer(g):
        return (y * 4 + zc_of(jnp.int32(g)), t)

    def t_of(r):
        return lax.rem(z_lo + r // 4, 2) * 4 + lax.rem(x + r % 4, 4)

    def tpeer(r):
        return (c, t_of(r))

    def cpeer(k):
        return (lax.rem(y + k // 4, 4) * 4 + zc_of(jnp.int32(k % 4)), t)

    c_order = (11, 10, 7, 15, 6, 14, 9, 8, 3, 2, 5, 13, 4, 12, 1)
    y_order = (2, 1, 3)
    z_order = (3, 2, 1)
    t_order = (6, 5, 7, 2, 4, 1, 3)

    names = (
        "past", "new1", "new2", "new3", "ids", "q", "e1", "e2", "e3", "relk", "relv",
        "part", "stats", "dpart", "wo", "woz", "wof", "swap", "att", "datt", "rs2", "ar2", "ag2",
    )

    def remote(name, src, dst, peer):
        at = names.index(name)
        return pltpu.make_async_remote_copy(
            src_ref=src, dst_ref=dst, send_sem=ssem.at[at], recv_sem=rsem.at[at],
            device_id=peer, device_id_type=MESH,
        )

    def arrived(name, whole):
        remote(name, whole, whole, tpeer(1)).wait_recv()

    def sent(name, whole):
        remote(name, whole, whole, tpeer(1)).wait_send()

    barrier = pltpu.get_barrier_semaphore()
    for r in range(1, 4):
        pl.semaphore_signal(barrier, 1, device_id=ypeer(r), device_id_type=MESH)
    for r in range(1, 4):
        pl.semaphore_signal(barrier, 1, device_id=zpeer(r), device_id_type=MESH)
    for r in range(1, 8):
        pl.semaphore_signal(barrier, 1, device_id=tpeer(r), device_id_type=MESH)

    my_half = pl.ds(pl.multiple_of(core * 64, 64), 64)
    loads = {}
    todo = [
        ("x", x_hbm, x_v), ("ag", ag_hbm, ag_v),
        ("wk", wk_hbm, qkv_v.at[1]), ("wv", wv_hbm, qkv_v.at[2]), ("wq", wq_hbm, qkv_v.at[0]),
        ("pk", pk_hbm, past.at[0, pl.ds(0, 128)]), ("pv", pv_hbm, pv_v),
        ("seg", seg_hbm, idall.at[0, 0]), ("creq", creq_hbm, idall.at[0, 1]),
        ("emb", emb_hbm, emb_v), ("wo", wo_hbm.at[my_half], wo_full.at[t, core]), ("fg", fg_hbm, fg_v),
        ("wg", wg_hbm, ffn_v.at[0]), ("wu", wu_hbm, ffn_v.at[1]), ("wd", wd_hbm, ffn_v.at[2]),
        ("lg", lg_hbm, lg_v), ("lm", lm_hbm, lm_v),
    ]
    for i, (name, src, dst) in enumerate(todo):
        loads[name] = pltpu.make_async_copy(src, dst, lsem.at[i])
        loads[name].start()

    def gain_of(ref):
        return ref[...].astype(F32).reshape(1, 1024)

    loads["x"].wait()
    loads["ag"].wait()
    a_gain = gain_of(ag_v)
    normed = norm(x_v[...].astype(F32), a_gain)
    loads["wk"].wait()
    new[0, 0:128, :] = dot(normed, qkv_v[1]).astype(BF16)
    loads["wv"].wait()
    values = dot(normed, qkv_v[2])
    vrow[...] = values.astype(BF16)
    new[0, 128:256, :] = values.T.astype(BF16)
    loads["wq"].wait()
    queries = dot(normed, qkv_v[0]).astype(BF16).astype(F32) * 0.125
    qbuf[0] = queries.T.astype(BF16)
    loads["pk"].wait()
    loads["pv"].wait()
    past[0, 128:256, :] = pv_v[...].astype(F32).T.astype(BF16)
    loads["seg"].wait()
    loads["creq"].wait()

    first_row = (c * 8 + t) * 251
    row16 = lax.broadcasted_iota(jnp.int32, (16, 251), 0)
    col16 = lax.broadcasted_iota(jnp.int32, (16, 251), 1) + first_row
    wanted = jnp.full((16, 251), -1, jnp.int32)
    for q in range(4):
        wanted = jnp.where(row16 == q, ids_ref[q], wanted)
    one_hot = (col16 == wanted).astype(F32).astype(BF16)
    loads["emb"].wait()
    e1buf[0] = dot(one_hot, emb_v[...])[0:4].astype(BF16)
    pl.semaphore_wait(barrier, 13)

    for r in t_order:
        remote("e1", e1buf.at[0], e1buf.at[r], tpeer(r)).start()

    def send_new(d):
        remote("new%d" % d, new.at[0], new.at[d], ypeer(d)).start()

    for d in (2, 1):
        pl.when(y + d < 4)(lambda d=d: send_new(d))
    for g in z_order:
        remote("q", qbuf.at[0], qbuf.at[g], zpeer(g)).start()
    for d in y_order:
        remote("past", past.at[0], past.at[d], ypeer(d)).start()
    for d in y_order:
        remote("ids", idall.at[0], idall.at[d], ypeer(d)).start()
    for g in z_order:
        remote("ids", idall.at[0], idall.at[3 + g], zpeer(g)).start()

    remote("woz", wo_hbm.at[my_half], wo_full.at[t, core], tpeer(4)).start()
    for r in (2, 1, 3):
        remote("wo", wo_hbm.at[my_half], wo_full.at[t, core], tpeer(r)).start()

    my_columns = pl.ds(pl.multiple_of(t * 128, 128), 128)
    my_rows = pl.ds(pl.multiple_of(t * 16, 16), 16)

    def rows_of(r):
        return pl.ds(pl.multiple_of(t_of(r) * 16, 16), 16)

    for d in (2, 1):
        pl.when(y + d >= 4)(lambda d=d: send_new(d))
    send_new(3)
    for r in t_order:
        remote("relk", new.at[0, rows_of(r)], relk_ref.at[:, my_columns], tpeer(r)).start()
        remote("relv", vrow.at[rows_of(r)], relv_ref.at[:, my_columns], tpeer(r)).start()
    relk_ref[:, my_columns] = new[0, my_rows, :]
    relv_ref[:, my_columns] = vrow[my_rows, :]

    arrived("woz", wo_full.at[0, 0])
    across = t_of(4)
    for r in (2, 1, 3):
        remote("wof", wo_full.at[across, core], wo_full.at[across, core], tpeer(r)).start()

    arrived("ids", idall.at[pl.ds(1, 6)])
    new_ids = [idall[d, 0:1, :].astype(F32) for d in range(4)]
    past_ids = [idall[d, 1:2, :].astype(F32) for d in range(4)]
    id_columns = jnp.concatenate(
        new_ids + past_ids + [jnp.zeros((120, 128), F32)], axis=0).T
    for b in range(8):
        kid_s[b] = jnp.broadcast_to(id_columns[:, b : b + 1], (128, 128))
    idall[7] = idall[0]
    arrived("q", qbuf.at[pl.ds(1, 3)])
    arrived("e1", e1buf.at[pl.ds(1, 7)])
    e2buf[0] = sum(e1buf[r].astype(F32) for r in range(8)).astype(BF16)
    for k in c_order:
        remote("e2", e2buf.at[0], e2buf.at[k], cpeer(k)).start()

    pl.when(y >= 1)(lambda: arrived("new1", new.at[1]))
    pl.when(y >= 2)(lambda: arrived("new2", new.at[2]))
    arrived("past", past.at[pl.ds(1, 3)])

    def block(b):
        return new.at[b] if b < 4 else past.at[b - 4]

    k_iota = lax.broadcasted_iota(jnp.int32, (128, 128), 0)
    q_iota = lax.broadcasted_iota(jnp.int32, (128, 128), 1)

    def attend(i, _):
        g = 3 - i
        qt = qbuf[g]
        top = qt[0:64, :]
        low = qt[64:128, :]
        zero = jnp.zeros((64, 128), BF16)
        qd = jnp.concatenate(
            [jnp.concatenate([top, zero], axis=1), jnp.concatenate([zero, low], axis=1)], axis=0)
        qid = idall[4 + lax.rem(g + 3, 4), 0:1, :].astype(F32)
        q_at = y * 512 + zc_of(g) * 128

        def score(b):
            s = dot(block(b)[0:128, :], qd)
            ok = kid_s[b] == qid
            if b < 4:
                k_at = (y - b) * 512 + zc * 128
                ok = ok & (k_iota + (k_at - q_at) <= q_iota)
            s = jnp.where(jnp.concatenate([ok, ok], axis=1), s, NEG)
            s_s[b * 128 : (b + 1) * 128, :] = s
            return jnp.max(s.reshape(16, 8, 256), axis=0)

        def weigh(b, m):
            w = jnp.exp(s_s[b * 128 : (b + 1) * 128, :] - m)
            return jnp.sum(w.reshape(16, 8, 256), axis=0), dot(
                block(b)[128:256, :], w.astype(BF16))

        always = (0, 4, 5, 6, 7)
        highest = jnp.full((8, 256), FLOOR, F32)
        for b in always:
            highest = jnp.maximum(highest, score(b))
        hi_s[...] = highest

        def score_more(b):
            hi_s[...] = jnp.maximum(hi_s[...], score(b))

        pl.when(y >= 1)(lambda: score_more(1))
        pl.when(y >= 2)(lambda: score_more(2))
        m = jnp.max(hi_s[...], axis=0, keepdims=True)
        total_w = jnp.zeros((8, 256), F32)
        o = jnp.zeros((128, 256), F32)
        for b in always:
            more_w, more_o = weigh(b, m)
            total_w = total_w + more_w
            o = o + more_o
        tw_s[...] = total_w
        o_s[...] = o

        def weigh_more(b):
            more_w, more_o = weigh(b, m)
            tw_s[...] += more_w
            o_s[...] += more_o

        pl.when(y >= 1)(lambda: weigh_more(1))
        pl.when(y >= 2)(lambda: weigh_more(2))
        l = jnp.sum(tw_s[...], axis=0, keepdims=True)
        osend[g] = jnp.concatenate(
            [o_s[0:64, 0:128], o_s[64:128, 128:256]], axis=0).astype(BF16)
        stsend[g] = jnp.concatenate(
            [m[:, 0:128], m[:, 128:256], l[:, 0:128], l[:, 128:256], jnp.zeros((4, 128), F32)],
            axis=0)

        @pl.when(i < 3)
        def _():
            remote("part", osend.at[g], obuf.at[g], zpeer(g)).start()
            remote("stats", stsend.at[g], stbuf.at[g], zpeer(g)).start()

        return 0

    lax.fori_loop(0, 4, attend, 0)
    obuf[0] = osend[0]
    stbuf[0] = stsend[0]

    arrived("part", obuf.at[pl.ds(1, 3)])
    arrived("stats", stbuf.at[pl.ds(1, 3)])
    stats = [stbuf[f] for f in range(4)]
    tops = [st[0:2] for st in stats]
    joint = jnp.maximum(jnp.maximum(tops[0], tops[1]), jnp.maximum(tops[2], tops[3]))
    scales = [jnp.exp(m - joint) for m in tops]
    weight = sum(sc * st[2:4] for sc, st in zip(scales, stats))
    inverse = 1.0 / weight
    attended = jnp.zeros((128, 128), F32)
    for f in range(4):
        factor = scales[f] * inverse
        spread = jnp.concatenate(
            [jnp.broadcast_to(factor[0:1], (64, 128)), jnp.broadcast_to(factor[1:2], (64, 128))],
            axis=0)
        attended = attended + obuf[f].astype(F32) * spread
    abuf[:, my_columns] = attended.T.astype(BF16)
    for r in t_order:
        remote("att", abuf.at[:, my_columns], abuf.at[:, my_columns], tpeer(r)).start()

    arrived("e2", e2buf.at[pl.ds(1, 15)])
    embedded = sum(e2buf[k].astype(F32) for k in range(16))
    pl.when(y < 1)(lambda: arrived("new1", new.at[1]))
    pl.when(y < 2)(lambda: arrived("new2", new.at[2]))
    arrived("new3", new.at[3])

    def padded(rows):
        return jnp.concatenate([rows, jnp.zeros((12,) + rows.shape[1:], F32)], axis=0).astype(BF16)

    d_normed = padded(norm(embedded, a_gain).astype(F32))
    dq = dot(d_normed, qkv_v[0]).astype(BF16).astype(F32)[0:4] * 0.125
    dk = dot(d_normed, qkv_v[1]).astype(BF16).astype(F32)[0:4]
    dv = dot(d_normed, qkv_v[2]).astype(BF16).astype(F32)[0:4]
    lane4 = lax.broadcasted_iota(jnp.int32, (4, 128), 1)
    qd8 = jnp.concatenate(
        [jnp.where(lane4 < 64, dq, 0.0), jnp.where(lane4 >= 64, dq, 0.0)], axis=0)
    qd16 = jnp.concatenate([qd8, jnp.zeros((8, 128), F32)], axis=0).astype(BF16)
    k_ids = jnp.concatenate(new_ids + past_ids, axis=1)
    rid = (lax.broadcasted_iota(jnp.int32, (16, 1024), 0) % 4).astype(F32)
    s = jnp.concatenate([dot_nt(qd16, block(b)[0:128, :]) for b in range(8)], axis=1)
    s = jnp.where(rid == k_ids, s, NEG)
    m = jnp.maximum(jnp.max(s, axis=1, keepdims=True), FLOOR)
    w = jnp.exp(s - m)
    l = jnp.sum(w, axis=1, keepdims=True)
    w = w.astype(BF16)
    o = sum(
        dot_nt(w[:, b * 128 : (b + 1) * 128], block(b)[128:256, :]) for b in range(8))
    dbuf[0, 0:8, :] = o[0:8]
    dbuf[0, 8:16, :] = jnp.broadcast_to(m[0:8], (8, 128))
    dbuf[0, 16:24, :] = jnp.broadcast_to(l[0:8], (8, 128))
    for g in z_order:
        remote("dpart", dbuf.at[0], dbuf.at[g], zpeer(g)).start()

    arrived("wo", wo_full.at[pl.ds(0, 3), 0])
    arrived("wof", wo_full.at[pl.ds(0, 3), 0])
    loads["wo"].wait()
    remote("swap", wo_full.at[:, core], wo_full.at[:, core], zpeer(1)).start()

    def units(rows):
        gate = dot_nt(rows, ffn_v[0])
        up = dot_nt(rows, ffn_v[1])
        hidden = (jax.nn.gelu(gate, approximate=True) * up).astype(BF16)
        return dot(hidden, ffn_v[2])

    arrived("swap", wo_full.at[:, 0])
    arrived("att", abuf.at[:, pl.ds(0, 896)])
    residual = x_v[...].astype(F32) + dot(abuf[...], wo_full[...].reshape(1024, 1024))
    res_s[...] = residual

    own_m = jnp.sum(qd8 * jnp.concatenate([dk, dk], axis=0), axis=1, keepdims=True)
    own_m = jnp.broadcast_to(own_m, (8, 128))
    arrived("dpart", dbuf.at[pl.ds(1, 3)])
    dparts = [dbuf[e] for e in range(4)]
    joint = own_m
    for part in dparts:
        joint = jnp.maximum(joint, part[8:16])
    own_scale = jnp.exp(own_m - joint)
    weight = own_scale
    summed = own_scale * jnp.concatenate([dv, dv], axis=0)
    for part in dparts:
        scale = jnp.exp(part[8:16] - joint)
        weight = weight + scale * part[16:24]
        summed = summed + scale * part[0:8]
    summed = summed / weight
    d_attended = jnp.where(lane4 < 64, summed[0:4], summed[4:8])
    dabuf[t] = d_attended.astype(BF16)
    for r in t_order:
        remote("datt", dabuf.at[t], dabuf.at[t], tpeer(r)).start()

    loads["fg"].wait()
    f_gain = gain_of(fg_v)
    nbuf[...] = norm(residual, f_gain)
    loads["wg"].wait()
    loads["wu"].wait()
    loads["wd"].wait()
    part_s[...] = units(nbuf[...]).astype(BF16)
    for r in t_order:
        remote("rs2", part_s.at[rows_of(r)], rs2buf.at[r], tpeer(r)).start()

    arrived("datt", dabuf.at[pl.ds(0, 7)])
    d_all = jnp.concatenate([dabuf[i].astype(F32) for i in range(8)], axis=1)
    d_residual = embedded + dot(padded(d_all), wo_full[...].reshape(1024, 1024))[0:4]
    ar2buf[0] = units(padded(norm(d_residual, f_gain).astype(F32)))[0:4].astype(BF16)
    for r in t_order:
        remote("ar2", ar2buf.at[0], ar2buf.at[r], tpeer(r)).start()

    final = res_s[my_rows, :] + part_s[my_rows, :].astype(F32)
    arrived("rs2", rs2buf.at[pl.ds(1, 7)])
    for r in range(1, 8):
        final = final + rs2buf[r].astype(F32)
    out_ref[my_rows, :] = final.astype(BF16)
    for r in t_order:
        remote("ag2", out_ref.at[my_rows], out_ref.at[my_rows], tpeer(r)).start()

    arrived("ar2", ar2buf.at[pl.ds(1, 7)])
    d_final = d_residual + sum(ar2buf[r].astype(F32) for r in range(8))
    loads["lg"].wait()
    loads["lm"].wait()
    l_normed = padded(norm(d_final, gain_of(lg_v)).astype(F32))
    logits_ref[...] = dot(l_normed, lm_v[...])[0:4]

    arrived("relk", relk_ref.at[:, pl.ds(0, 896)])
    arrived("relv", relv_ref.at[:, pl.ds(0, 896)])
    for d in range(1, 4):
        sent("new%d" % d, new.at[d])
    sent("past", past.at[pl.ds(1, 3)])
    sent("ids", idall.at[pl.ds(1, 6)])
    sent("q", qbuf.at[pl.ds(1, 3)])
    sent("e1", e1buf.at[pl.ds(1, 7)])
    sent("e2", e2buf.at[pl.ds(1, 15)])
    sent("relk", relk_ref.at[:, pl.ds(0, 896)])
    sent("relv", relv_ref.at[:, pl.ds(0, 896)])
    sent("part", obuf.at[pl.ds(1, 3)])
    sent("stats", stbuf.at[pl.ds(1, 3)])
    sent("dpart", dbuf.at[pl.ds(1, 3)])
    sent("wo", wo_full.at[pl.ds(0, 3), 0])
    sent("woz", wo_full.at[0, 0])
    sent("wof", wo_full.at[pl.ds(0, 3), 0])
    sent("swap", wo_full.at[:, 0])
    sent("att", abuf.at[:, pl.ds(0, 896)])
    sent("datt", dabuf.at[pl.ds(0, 7)])
    sent("rs2", rs2buf.at[pl.ds(1, 7)])
    sent("ar2", ar2buf.at[pl.ds(1, 7)])
    arrived("ag2", out_ref.at[pl.ds(0, 112)])
    sent("ag2", out_ref.at[pl.ds(0, 112)])


def hand_over(*refs):
    sems = refs[8]
    copies = [pltpu.make_async_copy(refs[i], refs[4 + i], sems.at[i]) for i in range(4)]
    for copy in copies:
        copy.start()
    for copy in copies:
        copy.wait()


def on_device(
    prompt_states, segment_ids, past_keys, past_values, cache_request, decode_ids, embed_table,
    attn_gain, ff_gain, final_gain, w_query, w_key, w_value, w_out, w_gate, w_up, w_down, lm_head,
):
    in_hbm = pl.BlockSpec(memory_space=pltpu.HBM)
    in_vmem = pl.BlockSpec(memory_space=pltpu.VMEM)
    dma = pltpu.SemaphoreType.DMA
    local = [
        ((128, 1024), BF16), ((1024,), BF16), ((1024,), BF16), ((1024,), BF16),
        ((3, 1024, 128), BF16), ((3, 352, 1024), BF16), ((1024, 251), BF16),
        ((251, 1024), BF16), ((128, 128), BF16),
        ((128, 128), BF16), ((8, 128, 128), F32), ((1024, 256), F32), ((8, 256), F32),
        ((8, 256), F32), ((128, 256), F32), ((4, 128, 128), BF16), ((4, 8, 128), F32),
        ((128, 1024), BF16), ((128, 1024), BF16), ((128, 1024), F32),
    ]
    arriving = [
        ((4, 256, 128), BF16), ((4, 256, 128), BF16), ((8, 8, 128), jnp.int32),
        ((4, 128, 128), BF16), ((4, 128, 128), BF16), ((4, 8, 128), F32), ((4, 24, 128), F32),
        ((8, 4, 1024), BF16), ((16, 4, 1024), BF16), ((4, 4, 1024), BF16),
        ((8, 2, 64, 1024), BF16), ((128, 1024), BF16), ((8, 4, 128), BF16),
        ((8, 16, 1024), BF16), ((8, 4, 1024), BF16),
    ]
    shapes = [((128, 1024), BF16), ((4, 251), F32), ((16, 1024), BF16), ((16, 1024), BF16)]
    arrays = [
        pltpu.with_memory_space_constraint(a, pltpu.HBM)
        for a in (
            prompt_states, segment_ids, past_keys, past_values, cache_request, embed_table,
            attn_gain, ff_gain, final_gain, w_query, w_key, w_value, w_out, w_gate.T, w_up.T,
            w_down, lm_head,
        )
    ]
    results = pl.pallas_call(
        kernel,
        out_shape=tuple(pltpu.VMEM(s, d) for s, d in shapes),
        in_specs=[pl.BlockSpec(memory_space=pltpu.SMEM)] + [in_hbm] * 17,
        out_specs=(in_vmem,) * 4,
        scratch_shapes=[pltpu.VMEM(s, d) for s, d in local + arriving]
        + [dma((17,)), dma((23,)), dma((23,))],
        compiler_params=pltpu.CompilerParams(
            collective_id=0, has_side_effects=True, vmem_limit_bytes=60 * 1024 * 1024),
    )(decode_ids, *arrays)
    results = [pltpu.with_memory_space_constraint(a, pltpu.VMEM) for a in results]
    return pl.pallas_call(
        hand_over,
        out_shape=tuple(jax.ShapeDtypeStruct(s, d) for s, d in shapes),
        in_specs=[in_vmem] * 4,
        out_specs=(in_hbm,) * 4,
        scratch_shapes=[dma((4,))],
    )(*results)


def solution(mesh):
    placed = (
        P("ctx", None),
        P("ctx"),
        P("ctx", "tp"),
        P("ctx", "tp"),
        P("ctx"),
        P(),
        P(("ctx", "tp"), None),
        P(),
        P(),
        P(),
        P(None, "tp"),
        P(None, "tp"),
        P(None, "tp"),
        P("tp", None),
        P(None, "tp"),
        P(None, "tp"),
        P("tp", None),
        P(None, ("ctx", "tp")),
    )
    return jax.shard_map(
        on_device,
        mesh=mesh,
        in_specs=placed,
        out_specs=(
            P("ctx", None),
            P(None, ("ctx", "tp")),
            P(("ctx", "tp"), None),
            P(("ctx", "tp"), None),
        ),
        check_vma=False,
    )
```

```python
import jax
import jax.numpy as jnp
from jax import lax
from jax.experimental import pallas as pl
from jax.experimental.pallas import tpu as pltpu
from jax.sharding import PartitionSpec as P

DH = 64
EPS = 1e-06
NEG = -1e30
FLOOR = -1e29
MESH = pl.DeviceIdType.MESH
F32 = jnp.float32
BF16 = jnp.bfloat16


def dot(a, b):
    return jnp.dot(a, b, preferred_element_type=F32)


def dot_nt(a, b):
    return lax.dot_general(a, b, (((1,), (1,)), ((), ())), preferred_element_type=F32)


def norm(states, gain):
    mean_square = jnp.mean(states * states, axis=-1, keepdims=True)
    return (states * lax.rsqrt(mean_square + EPS) * gain).astype(BF16)


def kernel(
    ids_ref, x_hbm, seg_hbm, pk_hbm, pv_hbm, creq_hbm, emb_hbm,
    ag_hbm, fg_hbm, lg_hbm, wq_hbm, wk_hbm, wv_hbm, wo_hbm, wg_hbm, wu_hbm, wd_hbm, lm_hbm,
    out_ref, logits_ref, relk_ref, relv_ref,
    x_v, ag_v, fg_v, lg_v, qkv_v, ffn_v, lm_v, emb_v, pv_v,
    vrow, kid_s, s_s, hi_s, tw_s, o_s, osend, stsend, part_s, nbuf, res_s,
    past, new, idall, qbuf, obuf, stbuf, dbuf, e1buf, e2buf, e3buf,
    wo_full, abuf, dabuf, rs2buf, ar2buf,
    lsem, ssem, rsem,
):
    c = lax.axis_index("ctx")
    t = lax.axis_index("tp")
    y = lax.div(c, 4)
    zc = lax.rem(c, 4)
    z_hi = lax.div(zc, 2)
    core = lax.rem(c, 2)
    z_lo = lax.div(t, 4)
    x = lax.rem(t, 4)

    def ypeer(d):
        return (lax.rem(y + d, 4) * 4 + zc, t)

    def zc_of(g):
        return lax.rem(z_hi + lax.div(g, 2), 2) * 2 + lax.rem(core + lax.rem(g, 2), 2)

    def zpeer(g):
        return (y * 4 + zc_of(jnp.int32(g)), t)

    def t_of(r):
        return lax.rem(z_lo + r // 4, 2) * 4 + lax.rem(x + r % 4, 4)

    def tpeer(r):
        return (c, t_of(r))

    def cpeer(k):
        return (lax.rem(y + k // 4, 4) * 4 + zc_of(jnp.int32(k % 4)), t)

    c_order = (11, 10, 7, 15, 6, 14, 9, 8, 3, 2, 5, 13, 4, 12, 1)
    y_order = (2, 1, 3)
    z_order = (3, 2, 1)
    t_order = (6, 5, 7, 2, 4, 1, 3)

    names = (
        "past", "new1", "new2", "new3", "ids", "q", "e1", "e2", "e3", "relk", "relv",
        "part", "stats", "dpart", "wo", "woz", "wof", "swap", "att", "datt", "rs2a", "rs2b", "ar2", "ag2",
    )

    def remote(name, src, dst, peer):
        at = names.index(name)
        return pltpu.make_async_remote_copy(
            src_ref=src, dst_ref=dst, send_sem=ssem.at[at], recv_sem=rsem.at[at],
            device_id=peer, device_id_type=MESH,
        )

    def arrived(name, whole):
        remote(name, whole, whole, tpeer(1)).wait_recv()

    def sent(name, whole):
        remote(name, whole, whole, tpeer(1)).wait_send()

    barrier = pltpu.get_barrier_semaphore()
    for r in range(1, 4):
        pl.semaphore_signal(barrier, 1, device_id=ypeer(r), device_id_type=MESH)
    for r in range(1, 4):
        pl.semaphore_signal(barrier, 1, device_id=zpeer(r), device_id_type=MESH)
    for r in range(1, 8):
        pl.semaphore_signal(barrier, 1, device_id=tpeer(r), device_id_type=MESH)

    my_half = pl.ds(pl.multiple_of(core * 64, 64), 64)
    loads = {}
    todo = [
        ("x", x_hbm, x_v), ("ag", ag_hbm, ag_v),
        ("wk", wk_hbm, qkv_v.at[1]), ("wv", wv_hbm, qkv_v.at[2]), ("wq", wq_hbm, qkv_v.at[0]),
        ("pk", pk_hbm, past.at[0, pl.ds(0, 128)]), ("pv", pv_hbm, pv_v),
        ("seg", seg_hbm, idall.at[0, 0]), ("creq", creq_hbm, idall.at[0, 1]),
        ("emb", emb_hbm, emb_v), ("wo", wo_hbm.at[my_half], wo_full.at[t, core]), ("fg", fg_hbm, fg_v),
        ("wg", wg_hbm, ffn_v.at[0]), ("wu", wu_hbm, ffn_v.at[1]), ("wd", wd_hbm, ffn_v.at[2]),
        ("lg", lg_hbm, lg_v), ("lm", lm_hbm, lm_v),
    ]
    for i, (name, src, dst) in enumerate(todo):
        loads[name] = pltpu.make_async_copy(src, dst, lsem.at[i])
        loads[name].start()

    def gain_of(ref):
        return ref[...].astype(F32).reshape(1, 1024)

    loads["x"].wait()
    loads["ag"].wait()
    a_gain = gain_of(ag_v)
    normed = norm(x_v[...].astype(F32), a_gain)
    loads["wk"].wait()
    new[0, 0:128, :] = dot(normed, qkv_v[1]).astype(BF16)
    loads["wv"].wait()
    values = dot(normed, qkv_v[2])
    vrow[...] = values.astype(BF16)
    new[0, 128:256, :] = values.T.astype(BF16)
    loads["wq"].wait()
    queries = dot(normed, qkv_v[0]).astype(BF16).astype(F32) * 0.125
    qbuf[0] = queries.T.astype(BF16)
    loads["pk"].wait()
    loads["pv"].wait()
    past[0, 128:256, :] = pv_v[...].astype(F32).T.astype(BF16)
    loads["seg"].wait()
    loads["creq"].wait()

    first_row = (c * 8 + t) * 251
    row16 = lax.broadcasted_iota(jnp.int32, (16, 251), 0)
    col16 = lax.broadcasted_iota(jnp.int32, (16, 251), 1) + first_row
    wanted = jnp.full((16, 251), -1, jnp.int32)
    for q in range(4):
        wanted = jnp.where(row16 == q, ids_ref[q], wanted)
    one_hot = (col16 == wanted).astype(F32).astype(BF16)
    loads["emb"].wait()
    e1buf[0] = dot(one_hot, emb_v[...])[0:4].astype(BF16)
    pl.semaphore_wait(barrier, 13)

    for r in t_order:
        remote("e1", e1buf.at[0], e1buf.at[r], tpeer(r)).start()

    def send_new(d):
        remote("new%d" % d, new.at[0], new.at[d], ypeer(d)).start()

    for d in (2, 1):
        pl.when(y + d < 4)(lambda d=d: send_new(d))
    for g in z_order:
        remote("q", qbuf.at[0], qbuf.at[g], zpeer(g)).start()
    for d in y_order:
        remote("past", past.at[0], past.at[d], ypeer(d)).start()
    for d in y_order:
        remote("ids", idall.at[0], idall.at[d], ypeer(d)).start()
    for g in z_order:
        remote("ids", idall.at[0], idall.at[3 + g], zpeer(g)).start()

    remote("woz", wo_hbm.at[my_half], wo_full.at[t, core], tpeer(4)).start()
    for r in (2, 1, 3):
        remote("wo", wo_hbm.at[my_half], wo_full.at[t, core], tpeer(r)).start()

    my_columns = pl.ds(pl.multiple_of(t * 128, 128), 128)
    my_rows = pl.ds(pl.multiple_of(t * 16, 16), 16)

    def rows_of(r):
        return pl.ds(pl.multiple_of(t_of(r) * 16, 16), 16)

    for d in (2, 1):
        pl.when(y + d >= 4)(lambda d=d: send_new(d))
    send_new(3)
    for r in t_order:
        remote("relk", new.at[0, rows_of(r)], relk_ref.at[:, my_columns], tpeer(r)).start()
        remote("relv", vrow.at[rows_of(r)], relv_ref.at[:, my_columns], tpeer(r)).start()
    relk_ref[:, my_columns] = new[0, my_rows, :]
    relv_ref[:, my_columns] = vrow[my_rows, :]

    arrived("woz", wo_full.at[0, 0])
    across = t_of(4)
    for r in (2, 1, 3):
        remote("wof", wo_full.at[across, core], wo_full.at[across, core], tpeer(r)).start()

    arrived("ids", idall.at[pl.ds(1, 6)])
    new_ids = [idall[d, 0:1, :].astype(F32) for d in range(4)]
    past_ids = [idall[d, 1:2, :].astype(F32) for d in range(4)]
    id_columns = jnp.concatenate(
        new_ids + past_ids + [jnp.zeros((120, 128), F32)], axis=0).T
    for b in range(8):
        kid_s[b] = jnp.broadcast_to(id_columns[:, b : b + 1], (128, 128))
    idall[7] = idall[0]
    arrived("q", qbuf.at[pl.ds(1, 3)])
    arrived("e1", e1buf.at[pl.ds(1, 7)])
    e2buf[0] = sum(e1buf[r].astype(F32) for r in range(8)).astype(BF16)
    for k in c_order:
        remote("e2", e2buf.at[0], e2buf.at[k], cpeer(k)).start()

    pl.when(y >= 1)(lambda: arrived("new1", new.at[1]))
    pl.when(y >= 2)(lambda: arrived("new2", new.at[2]))
    arrived("past", past.at[pl.ds(1, 3)])

    def block(b):
        return new.at[b] if b < 4 else past.at[b - 4]

    k_iota = lax.broadcasted_iota(jnp.int32, (128, 128), 0)
    q_iota = lax.broadcasted_iota(jnp.int32, (128, 128), 1)

    def attend(i, _):
        g = 3 - i
        qt = qbuf[g]
        top = qt[0:64, :]
        low = qt[64:128, :]
        zero = jnp.zeros((64, 128), BF16)
        qd = jnp.concatenate(
            [jnp.concatenate([top, zero], axis=1), jnp.concatenate([zero, low], axis=1)], axis=0)
        qid = idall[4 + lax.rem(g + 3, 4), 0:1, :].astype(F32)
        q_at = y * 512 + zc_of(g) * 128

        def score(b):
            s = dot(block(b)[0:128, :], qd)
            ok = kid_s[b] == qid
            if b < 4:
                k_at = (y - b) * 512 + zc * 128
                ok = ok & (k_iota + (k_at - q_at) <= q_iota)
            s = jnp.where(jnp.concatenate([ok, ok], axis=1), s, NEG)
            s_s[b * 128 : (b + 1) * 128, :] = s
            return jnp.max(s.reshape(16, 8, 256), axis=0)

        def weigh(b, m):
            w = jnp.exp(s_s[b * 128 : (b + 1) * 128, :] - m)
            return jnp.sum(w.reshape(16, 8, 256), axis=0), dot(
                block(b)[128:256, :], w.astype(BF16))

        always = (0, 4, 5, 6, 7)
        highest = jnp.full((8, 256), FLOOR, F32)
        for b in always:
            highest = jnp.maximum(highest, score(b))
        hi_s[...] = highest

        def score_more(b):
            hi_s[...] = jnp.maximum(hi_s[...], score(b))

        pl.when(y >= 1)(lambda: score_more(1))
        pl.when(y >= 2)(lambda: score_more(2))
        m = jnp.max(hi_s[...], axis=0, keepdims=True)
        total_w = jnp.zeros((8, 256), F32)
        o = jnp.zeros((128, 256), F32)
        for b in always:
            more_w, more_o = weigh(b, m)
            total_w = total_w + more_w
            o = o + more_o
        tw_s[...] = total_w
        o_s[...] = o

        def weigh_more(b):
            more_w, more_o = weigh(b, m)
            tw_s[...] += more_w
            o_s[...] += more_o

        pl.when(y >= 1)(lambda: weigh_more(1))
        pl.when(y >= 2)(lambda: weigh_more(2))
        l = jnp.sum(tw_s[...], axis=0, keepdims=True)
        osend[g] = jnp.concatenate(
            [o_s[0:64, 0:128], o_s[64:128, 128:256]], axis=0).astype(BF16)
        stsend[g] = jnp.concatenate(
            [m[:, 0:128], m[:, 128:256], l[:, 0:128], l[:, 128:256], jnp.zeros((4, 128), F32)],
            axis=0)

        @pl.when(i < 3)
        def _():
            remote("part", osend.at[g], obuf.at[g], zpeer(g)).start()
            remote("stats", stsend.at[g], stbuf.at[g], zpeer(g)).start()

        return 0

    lax.fori_loop(0, 4, attend, 0)
    obuf[0] = osend[0]
    stbuf[0] = stsend[0]

    arrived("part", obuf.at[pl.ds(1, 3)])
    arrived("stats", stbuf.at[pl.ds(1, 3)])
    stats = [stbuf[f] for f in range(4)]
    tops = [st[0:2] for st in stats]
    joint = jnp.maximum(jnp.maximum(tops[0], tops[1]), jnp.maximum(tops[2], tops[3]))
    scales = [jnp.exp(m - joint) for m in tops]
    weight = sum(sc * st[2:4] for sc, st in zip(scales, stats))
    inverse = 1.0 / weight
    attended = jnp.zeros((128, 128), F32)
    for f in range(4):
        factor = scales[f] * inverse
        spread = jnp.concatenate(
            [jnp.broadcast_to(factor[0:1], (64, 128)), jnp.broadcast_to(factor[1:2], (64, 128))],
            axis=0)
        attended = attended + obuf[f].astype(F32) * spread
    abuf[:, my_columns] = attended.T.astype(BF16)
    for r in t_order:
        remote("att", abuf.at[:, my_columns], abuf.at[:, my_columns], tpeer(r)).start()

    arrived("e2", e2buf.at[pl.ds(1, 15)])
    embedded = sum(e2buf[k].astype(F32) for k in range(16))
    pl.when(y < 1)(lambda: arrived("new1", new.at[1]))
    pl.when(y < 2)(lambda: arrived("new2", new.at[2]))
    arrived("new3", new.at[3])

    def padded(rows):
        return jnp.concatenate([rows, jnp.zeros((12,) + rows.shape[1:], F32)], axis=0).astype(BF16)

    d_normed = padded(norm(embedded, a_gain).astype(F32))
    dq = dot(d_normed, qkv_v[0]).astype(BF16).astype(F32)[0:4] * 0.125
    dk = dot(d_normed, qkv_v[1]).astype(BF16).astype(F32)[0:4]
    dv = dot(d_normed, qkv_v[2]).astype(BF16).astype(F32)[0:4]
    lane4 = lax.broadcasted_iota(jnp.int32, (4, 128), 1)
    qd8 = jnp.concatenate(
        [jnp.where(lane4 < 64, dq, 0.0), jnp.where(lane4 >= 64, dq, 0.0)], axis=0)
    qd16 = jnp.concatenate([qd8, jnp.zeros((8, 128), F32)], axis=0).astype(BF16)
    k_ids = jnp.concatenate(new_ids + past_ids, axis=1)
    rid = (lax.broadcasted_iota(jnp.int32, (16, 1024), 0) % 4).astype(F32)
    s = jnp.concatenate([dot_nt(qd16, block(b)[0:128, :]) for b in range(8)], axis=1)
    s = jnp.where(rid == k_ids, s, NEG)
    m = jnp.maximum(jnp.max(s, axis=1, keepdims=True), FLOOR)
    w = jnp.exp(s - m)
    l = jnp.sum(w, axis=1, keepdims=True)
    w = w.astype(BF16)
    o = sum(
        dot_nt(w[:, b * 128 : (b + 1) * 128], block(b)[128:256, :]) for b in range(8))
    dbuf[0, 0:8, :] = o[0:8]
    dbuf[0, 8:16, :] = jnp.broadcast_to(m[0:8], (8, 128))
    dbuf[0, 16:24, :] = jnp.broadcast_to(l[0:8], (8, 128))
    for g in z_order:
        remote("dpart", dbuf.at[0], dbuf.at[g], zpeer(g)).start()

    arrived("wo", wo_full.at[pl.ds(0, 3), 0])
    arrived("wof", wo_full.at[pl.ds(0, 3), 0])
    loads["wo"].wait()
    remote("swap", wo_full.at[:, core], wo_full.at[:, core], zpeer(1)).start()

    half = (pl.ds(0, 512), pl.ds(512, 512))
    def hidden_of(rows):
        gate = dot_nt(rows, ffn_v[0])
        up = dot_nt(rows, ffn_v[1])
        return (jax.nn.gelu(gate, approximate=True) * up).astype(BF16)

    def units(rows):
        return dot(hidden_of(rows), ffn_v[2])

    arrived("swap", wo_full.at[:, 0])
    arrived("att", abuf.at[:, pl.ds(0, 896)])
    residual = x_v[...].astype(F32) + dot(abuf[...], wo_full[...].reshape(1024, 1024))
    res_s[...] = residual

    own_m = jnp.sum(qd8 * jnp.concatenate([dk, dk], axis=0), axis=1, keepdims=True)
    own_m = jnp.broadcast_to(own_m, (8, 128))
    arrived("dpart", dbuf.at[pl.ds(1, 3)])
    dparts = [dbuf[e] for e in range(4)]
    joint = own_m
    for part in dparts:
        joint = jnp.maximum(joint, part[8:16])
    own_scale = jnp.exp(own_m - joint)
    weight = own_scale
    summed = own_scale * jnp.concatenate([dv, dv], axis=0)
    for part in dparts:
        scale = jnp.exp(part[8:16] - joint)
        weight = weight + scale * part[16:24]
        summed = summed + scale * part[0:8]
    summed = summed / weight
    d_attended = jnp.where(lane4 < 64, summed[0:4], summed[4:8])
    dabuf[t] = d_attended.astype(BF16)
    for r in t_order:
        remote("datt", dabuf.at[t], dabuf.at[t], tpeer(r)).start()

    loads["fg"].wait()
    f_gain = gain_of(fg_v)
    nbuf[...] = norm(residual, f_gain)
    loads["wg"].wait()
    loads["wu"].wait()
    loads["wd"].wait()
    hidden = hidden_of(nbuf[...])
    for h in range(2):
        part_s[:, half[h]] = dot(hidden, ffn_v[2, :, half[h]]).astype(BF16)
        for r in t_order:
            remote("rs2" + "ab"[h], part_s.at[rows_of(r), half[h]], rs2buf.at[r, :, half[h]],
                   tpeer(r)).start()

    arrived("datt", dabuf.at[pl.ds(0, 7)])
    d_all = jnp.concatenate([dabuf[i].astype(F32) for i in range(8)], axis=1)
    d_residual = embedded + dot(padded(d_all), wo_full[...].reshape(1024, 1024))[0:4]
    ar2buf[0] = units(padded(norm(d_residual, f_gain).astype(F32)))[0:4].astype(BF16)
    for r in t_order:
        remote("ar2", ar2buf.at[0], ar2buf.at[r], tpeer(r)).start()

    for h in range(2):
        final = res_s[my_rows, half[h]] + part_s[my_rows, half[h]].astype(F32)
        arrived("rs2" + "ab"[h], rs2buf.at[pl.ds(1, 7), :, half[h]])
        for r in range(1, 8):
            final = final + rs2buf[r, :, half[h]].astype(F32)
        out_ref[my_rows, half[h]] = final.astype(BF16)
        for r in t_order:
            remote("ag2", out_ref.at[my_rows, half[h]], out_ref.at[my_rows, half[h]],
                   tpeer(r)).start()

    arrived("ar2", ar2buf.at[pl.ds(1, 7)])
    d_final = d_residual + sum(ar2buf[r].astype(F32) for r in range(8))
    loads["lg"].wait()
    loads["lm"].wait()
    l_normed = padded(norm(d_final, gain_of(lg_v)).astype(F32))
    logits_ref[...] = dot(l_normed, lm_v[...])[0:4]

    arrived("relk", relk_ref.at[:, pl.ds(0, 896)])
    arrived("relv", relv_ref.at[:, pl.ds(0, 896)])
    for d in range(1, 4):
        sent("new%d" % d, new.at[d])
    sent("past", past.at[pl.ds(1, 3)])
    sent("ids", idall.at[pl.ds(1, 6)])
    sent("q", qbuf.at[pl.ds(1, 3)])
    sent("e1", e1buf.at[pl.ds(1, 7)])
    sent("e2", e2buf.at[pl.ds(1, 15)])
    sent("relk", relk_ref.at[:, pl.ds(0, 896)])
    sent("relv", relv_ref.at[:, pl.ds(0, 896)])
    sent("part", obuf.at[pl.ds(1, 3)])
    sent("stats", stbuf.at[pl.ds(1, 3)])
    sent("dpart", dbuf.at[pl.ds(1, 3)])
    sent("wo", wo_full.at[pl.ds(0, 3), 0])
    sent("woz", wo_full.at[0, 0])
    sent("wof", wo_full.at[pl.ds(0, 3), 0])
    sent("swap", wo_full.at[:, 0])
    sent("att", abuf.at[:, pl.ds(0, 896)])
    sent("datt", dabuf.at[pl.ds(0, 7)])
    sent("rs2a", rs2buf.at[pl.ds(1, 7), :, half[0]])
    sent("rs2b", rs2buf.at[pl.ds(1, 7), :, half[1]])
    sent("ar2", ar2buf.at[pl.ds(1, 7)])
    arrived("ag2", out_ref.at[pl.ds(0, 112)])
    sent("ag2", out_ref.at[pl.ds(0, 112)])


def hand_over(*refs):
    sems = refs[8]
    copies = [pltpu.make_async_copy(refs[i], refs[4 + i], sems.at[i]) for i in range(4)]
    for copy in copies:
        copy.start()
    for copy in copies:
        copy.wait()


def on_device(
    prompt_states, segment_ids, past_keys, past_values, cache_request, decode_ids, embed_table,
    attn_gain, ff_gain, final_gain, w_query, w_key, w_value, w_out, w_gate, w_up, w_down, lm_head,
):
    in_hbm = pl.BlockSpec(memory_space=pltpu.HBM)
    in_vmem = pl.BlockSpec(memory_space=pltpu.VMEM)
    dma = pltpu.SemaphoreType.DMA
    local = [
        ((128, 1024), BF16), ((1024,), BF16), ((1024,), BF16), ((1024,), BF16),
        ((3, 1024, 128), BF16), ((3, 352, 1024), BF16), ((1024, 251), BF16),
        ((251, 1024), BF16), ((128, 128), BF16),
        ((128, 128), BF16), ((8, 128, 128), F32), ((1024, 256), F32), ((8, 256), F32),
        ((8, 256), F32), ((128, 256), F32), ((4, 128, 128), BF16), ((4, 8, 128), F32),
        ((128, 1024), BF16), ((128, 1024), BF16), ((128, 1024), F32),
    ]
    arriving = [
        ((4, 256, 128), BF16), ((4, 256, 128), BF16), ((8, 8, 128), jnp.int32),
        ((4, 128, 128), BF16), ((4, 128, 128), BF16), ((4, 8, 128), F32), ((4, 24, 128), F32),
        ((8, 4, 1024), BF16), ((16, 4, 1024), BF16), ((4, 4, 1024), BF16),
        ((8, 2, 64, 1024), BF16), ((128, 1024), BF16), ((8, 4, 128), BF16),
        ((8, 16, 1024), BF16), ((8, 4, 1024), BF16),
    ]
    shapes = [((128, 1024), BF16), ((4, 251), F32), ((16, 1024), BF16), ((16, 1024), BF16)]
    arrays = [
        pltpu.with_memory_space_constraint(a, pltpu.HBM)
        for a in (
            prompt_states, segment_ids, past_keys, past_values, cache_request, embed_table,
            attn_gain, ff_gain, final_gain, w_query, w_key, w_value, w_out, w_gate.T, w_up.T,
            w_down, lm_head,
        )
    ]
    results = pl.pallas_call(
        kernel,
        out_shape=tuple(pltpu.VMEM(s, d) for s, d in shapes),
        in_specs=[pl.BlockSpec(memory_space=pltpu.SMEM)] + [in_hbm] * 17,
        out_specs=(in_vmem,) * 4,
        scratch_shapes=[pltpu.VMEM(s, d) for s, d in local + arriving]
        + [dma((17,)), dma((24,)), dma((24,))],
        compiler_params=pltpu.CompilerParams(
            collective_id=0, has_side_effects=True, vmem_limit_bytes=60 * 1024 * 1024),
    )(decode_ids, *arrays)
    results = [pltpu.with_memory_space_constraint(a, pltpu.VMEM) for a in results]
    return pl.pallas_call(
        hand_over,
        out_shape=tuple(jax.ShapeDtypeStruct(s, d) for s, d in shapes),
        in_specs=[in_vmem] * 4,
        out_specs=(in_hbm,) * 4,
        scratch_shapes=[dma((4,))],
    )(*results)


def solution(mesh):
    placed = (
        P("ctx", None),
        P("ctx"),
        P("ctx", "tp"),
        P("ctx", "tp"),
        P("ctx"),
        P(),
        P(("ctx", "tp"), None),
        P(),
        P(),
        P(),
        P(None, "tp"),
        P(None, "tp"),
        P(None, "tp"),
        P("tp", None),
        P(None, "tp"),
        P(None, "tp"),
        P("tp", None),
        P(None, ("ctx", "tp")),
    )
    return jax.shard_map(
        on_device,
        mesh=mesh,
        in_specs=placed,
        out_specs=(
            P("ctx", None),
            P(None, ("ctx", "tp")),
            P(("ctx", "tp"), None),
            P(("ctx", "tp"), None),
        ),
        check_vma=False,
    )
```

```python
import jax
import jax.numpy as jnp
from jax import lax
from jax.experimental import pallas as pl
from jax.experimental.pallas import tpu as pltpu
from jax.sharding import PartitionSpec as P

DH = 64
EPS = 1e-06
NEG = -1e30
FLOOR = -1e29
MESH = pl.DeviceIdType.MESH
F32 = jnp.float32
BF16 = jnp.bfloat16


def dot(a, b):
    return jnp.dot(a, b, preferred_element_type=F32)


def dot_nt(a, b):
    return lax.dot_general(a, b, (((1,), (1,)), ((), ())), preferred_element_type=F32)


def norm(states, gain):
    mean_square = jnp.mean(states * states, axis=-1, keepdims=True)
    return (states * lax.rsqrt(mean_square + EPS) * gain).astype(BF16)


def kernel(
    ids_ref, x_hbm, seg_hbm, pk_hbm, pv_hbm, creq_hbm, emb_hbm,
    ag_hbm, fg_hbm, lg_hbm, wq_hbm, wk_hbm, wv_hbm, wo_hbm, wg_hbm, wu_hbm, wd_hbm, lm_hbm,
    out_ref, logits_ref, relk_ref, relv_ref,
    x_v, ag_v, fg_v, lg_v, qkv_v, ffn_v, lm_v, emb_v, pv_v,
    vrow, kid_s, s_s, hi_s, tw_s, o_s, osend, stsend, part_s, nbuf, res_s,
    past, new, idall, qbuf, obuf, stbuf, dbuf, e1buf, e2buf, e3buf,
    wo_full, abuf, dabuf, rs2buf, ar2buf,
    lsem, ssem, rsem,
):
    c = lax.axis_index("ctx")
    t = lax.axis_index("tp")
    y = lax.div(c, 4)
    zc = lax.rem(c, 4)
    z_hi = lax.div(zc, 2)
    core = lax.rem(c, 2)
    z_lo = lax.div(t, 4)
    x = lax.rem(t, 4)

    def ypeer(d):
        return (lax.rem(y + d, 4) * 4 + zc, t)

    def zc_of(g):
        return lax.rem(z_hi + lax.div(g, 2), 2) * 2 + lax.rem(core + lax.rem(g, 2), 2)

    def zpeer(g):
        return (y * 4 + zc_of(jnp.int32(g)), t)

    def t_of(r):
        return lax.rem(z_lo + r // 4, 2) * 4 + lax.rem(x + r % 4, 4)

    def tpeer(r):
        return (c, t_of(r))

    def cpeer(k):
        return (lax.rem(y + k // 4, 4) * 4 + zc_of(jnp.int32(k % 4)), t)

    c_order = (11, 10, 7, 15, 6, 14, 9, 8, 3, 2, 5, 13, 4, 12, 1)
    y_order = (2, 1, 3)
    z_order = (3, 2, 1)
    t_order = (6, 5, 7, 2, 4, 1, 3)

    names = (
        "past", "new1", "new2", "new3", "ids", "q", "e1", "e2", "e3", "relk", "relv",
        "part", "stats", "dpart", "wo", "woz", "wof", "swap", "att", "datt", "rs2a", "rs2b", "rs2c", "rs2d", "ar2", "ag2",
    )

    def remote(name, src, dst, peer):
        at = names.index(name)
        return pltpu.make_async_remote_copy(
            src_ref=src, dst_ref=dst, send_sem=ssem.at[at], recv_sem=rsem.at[at],
            device_id=peer, device_id_type=MESH,
        )

    def arrived(name, whole):
        remote(name, whole, whole, tpeer(1)).wait_recv()

    def sent(name, whole):
        remote(name, whole, whole, tpeer(1)).wait_send()

    barrier = pltpu.get_barrier_semaphore()
    for r in range(1, 4):
        pl.semaphore_signal(barrier, 1, device_id=ypeer(r), device_id_type=MESH)
    for r in range(1, 4):
        pl.semaphore_signal(barrier, 1, device_id=zpeer(r), device_id_type=MESH)
    for r in range(1, 8):
        pl.semaphore_signal(barrier, 1, device_id=tpeer(r), device_id_type=MESH)

    my_half = pl.ds(pl.multiple_of(core * 64, 64), 64)
    loads = {}
    todo = [
        ("x", x_hbm, x_v), ("ag", ag_hbm, ag_v),
        ("wk", wk_hbm, qkv_v.at[1]), ("wv", wv_hbm, qkv_v.at[2]), ("wq", wq_hbm, qkv_v.at[0]),
        ("pk", pk_hbm, past.at[0, pl.ds(0, 128)]), ("pv", pv_hbm, pv_v),
        ("seg", seg_hbm, idall.at[0, 0]), ("creq", creq_hbm, idall.at[0, 1]),
        ("emb", emb_hbm, emb_v), ("wo", wo_hbm.at[my_half], wo_full.at[t, core]), ("fg", fg_hbm, fg_v),
        ("wg", wg_hbm, ffn_v.at[0]), ("wu", wu_hbm, ffn_v.at[1]), ("wd", wd_hbm, ffn_v.at[2]),
        ("lg", lg_hbm, lg_v), ("lm", lm_hbm, lm_v),
    ]
    for i, (name, src, dst) in enumerate(todo):
        loads[name] = pltpu.make_async_copy(src, dst, lsem.at[i])
        loads[name].start()

    def gain_of(ref):
        return ref[...].astype(F32).reshape(1, 1024)

    loads["x"].wait()
    loads["ag"].wait()
    a_gain = gain_of(ag_v)
    normed = norm(x_v[...].astype(F32), a_gain)
    loads["wk"].wait()
    new[0, 0:128, :] = dot(normed, qkv_v[1]).astype(BF16)
    loads["wv"].wait()
    values = dot(normed, qkv_v[2])
    vrow[...] = values.astype(BF16)
    new[0, 128:256, :] = values.T.astype(BF16)
    loads["wq"].wait()
    queries = dot(normed, qkv_v[0]).astype(BF16).astype(F32) * 0.125
    qbuf[0] = queries.T.astype(BF16)
    loads["pk"].wait()
    loads["pv"].wait()
    past[0, 128:256, :] = pv_v[...].astype(F32).T.astype(BF16)
    loads["seg"].wait()
    loads["creq"].wait()

    first_row = (c * 8 + t) * 251
    row16 = lax.broadcasted_iota(jnp.int32, (16, 251), 0)
    col16 = lax.broadcasted_iota(jnp.int32, (16, 251), 1) + first_row
    wanted = jnp.full((16, 251), -1, jnp.int32)
    for q in range(4):
        wanted = jnp.where(row16 == q, ids_ref[q], wanted)
    one_hot = (col16 == wanted).astype(F32).astype(BF16)
    loads["emb"].wait()
    e1buf[0] = dot(one_hot, emb_v[...])[0:4].astype(BF16)
    pl.semaphore_wait(barrier, 13)

    for r in t_order:
        remote("e1", e1buf.at[0], e1buf.at[r], tpeer(r)).start()

    def send_new(d):
        remote("new%d" % d, new.at[0], new.at[d], ypeer(d)).start()

    for d in (2, 1):
        pl.when(y + d < 4)(lambda d=d: send_new(d))
    for g in z_order:
        remote("q", qbuf.at[0], qbuf.at[g], zpeer(g)).start()
    for d in y_order:
        remote("past", past.at[0], past.at[d], ypeer(d)).start()
    for d in y_order:
        remote("ids", idall.at[0], idall.at[d], ypeer(d)).start()
    for g in z_order:
        remote("ids", idall.at[0], idall.at[3 + g], zpeer(g)).start()

    remote("woz", wo_hbm.at[my_half], wo_full.at[t, core], tpeer(4)).start()
    for r in (2, 1, 3):
        remote("wo", wo_hbm.at[my_half], wo_full.at[t, core], tpeer(r)).start()

    my_columns = pl.ds(pl.multiple_of(t * 128, 128), 128)
    my_rows = pl.ds(pl.multiple_of(t * 16, 16), 16)

    def rows_of(r):
        return pl.ds(pl.multiple_of(t_of(r) * 16, 16), 16)

    for d in (2, 1):
        pl.when(y + d >= 4)(lambda d=d: send_new(d))
    send_new(3)
    for r in t_order:
        remote("relk", new.at[0, rows_of(r)], relk_ref.at[:, my_columns], tpeer(r)).start()
        remote("relv", vrow.at[rows_of(r)], relv_ref.at[:, my_columns], tpeer(r)).start()
    relk_ref[:, my_columns] = new[0, my_rows, :]
    relv_ref[:, my_columns] = vrow[my_rows, :]

    arrived("woz", wo_full.at[0, 0])
    across = t_of(4)
    for r in (2, 1, 3):
        remote("wof", wo_full.at[across, core], wo_full.at[across, core], tpeer(r)).start()

    arrived("ids", idall.at[pl.ds(1, 6)])
    new_ids = [idall[d, 0:1, :].astype(F32) for d in range(4)]
    past_ids = [idall[d, 1:2, :].astype(F32) for d in range(4)]
    id_columns = jnp.concatenate(
        new_ids + past_ids + [jnp.zeros((120, 128), F32)], axis=0).T
    for b in range(8):
        kid_s[b] = jnp.broadcast_to(id_columns[:, b : b + 1], (128, 128))
    idall[7] = idall[0]
    arrived("q", qbuf.at[pl.ds(1, 3)])
    arrived("e1", e1buf.at[pl.ds(1, 7)])
    e2buf[0] = sum(e1buf[r].astype(F32) for r in range(8)).astype(BF16)
    for k in c_order:
        remote("e2", e2buf.at[0], e2buf.at[k], cpeer(k)).start()

    pl.when(y >= 1)(lambda: arrived("new1", new.at[1]))
    pl.when(y >= 2)(lambda: arrived("new2", new.at[2]))
    arrived("past", past.at[pl.ds(1, 3)])

    def block(b):
        return new.at[b] if b < 4 else past.at[b - 4]

    k_iota = lax.broadcasted_iota(jnp.int32, (128, 128), 0)
    q_iota = lax.broadcasted_iota(jnp.int32, (128, 128), 1)

    def attend(i, _):
        g = 3 - i
        qt = qbuf[g]
        top = qt[0:64, :]
        low = qt[64:128, :]
        zero = jnp.zeros((64, 128), BF16)
        qd = jnp.concatenate(
            [jnp.concatenate([top, zero], axis=1), jnp.concatenate([zero, low], axis=1)], axis=0)
        qid = idall[4 + lax.rem(g + 3, 4), 0:1, :].astype(F32)
        q_at = y * 512 + zc_of(g) * 128

        def score(b):
            s = dot(block(b)[0:128, :], qd)
            ok = kid_s[b] == qid
            if b < 4:
                k_at = (y - b) * 512 + zc * 128
                ok = ok & (k_iota + (k_at - q_at) <= q_iota)
            s = jnp.where(jnp.concatenate([ok, ok], axis=1), s, NEG)
            s_s[b * 128 : (b + 1) * 128, :] = s
            return jnp.max(s.reshape(16, 8, 256), axis=0)

        def weigh(b, m):
            w = jnp.exp(s_s[b * 128 : (b + 1) * 128, :] - m)
            return jnp.sum(w.reshape(16, 8, 256), axis=0), dot(
                block(b)[128:256, :], w.astype(BF16))

        always = (0, 4, 5, 6, 7)
        highest = jnp.full((8, 256), FLOOR, F32)
        for b in always:
            highest = jnp.maximum(highest, score(b))
        hi_s[...] = highest

        def score_more(b):
            hi_s[...] = jnp.maximum(hi_s[...], score(b))

        pl.when(y >= 1)(lambda: score_more(1))
        pl.when(y >= 2)(lambda: score_more(2))
        m = jnp.max(hi_s[...], axis=0, keepdims=True)
        total_w = jnp.zeros((8, 256), F32)
        o = jnp.zeros((128, 256), F32)
        for b in always:
            more_w, more_o = weigh(b, m)
            total_w = total_w + more_w
            o = o + more_o
        tw_s[...] = total_w
        o_s[...] = o

        def weigh_more(b):
            more_w, more_o = weigh(b, m)
            tw_s[...] += more_w
            o_s[...] += more_o

        pl.when(y >= 1)(lambda: weigh_more(1))
        pl.when(y >= 2)(lambda: weigh_more(2))
        l = jnp.sum(tw_s[...], axis=0, keepdims=True)
        osend[g] = jnp.concatenate(
            [o_s[0:64, 0:128], o_s[64:128, 128:256]], axis=0).astype(BF16)
        stsend[g] = jnp.concatenate(
            [m[:, 0:128], m[:, 128:256], l[:, 0:128], l[:, 128:256], jnp.zeros((4, 128), F32)],
            axis=0)

        @pl.when(i < 3)
        def _():
            remote("part", osend.at[g], obuf.at[g], zpeer(g)).start()
            remote("stats", stsend.at[g], stbuf.at[g], zpeer(g)).start()

        return 0

    lax.fori_loop(0, 4, attend, 0)
    obuf[0] = osend[0]
    stbuf[0] = stsend[0]

    arrived("part", obuf.at[pl.ds(1, 3)])
    arrived("stats", stbuf.at[pl.ds(1, 3)])
    stats = [stbuf[f] for f in range(4)]
    tops = [st[0:2] for st in stats]
    joint = jnp.maximum(jnp.maximum(tops[0], tops[1]), jnp.maximum(tops[2], tops[3]))
    scales = [jnp.exp(m - joint) for m in tops]
    weight = sum(sc * st[2:4] for sc, st in zip(scales, stats))
    inverse = 1.0 / weight
    attended = jnp.zeros((128, 128), F32)
    for f in range(4):
        factor = scales[f] * inverse
        spread = jnp.concatenate(
            [jnp.broadcast_to(factor[0:1], (64, 128)), jnp.broadcast_to(factor[1:2], (64, 128))],
            axis=0)
        attended = attended + obuf[f].astype(F32) * spread
    abuf[:, my_columns] = attended.T.astype(BF16)
    for r in t_order:
        remote("att", abuf.at[:, my_columns], abuf.at[:, my_columns], tpeer(r)).start()

    arrived("e2", e2buf.at[pl.ds(1, 15)])
    embedded = sum(e2buf[k].astype(F32) for k in range(16))
    pl.when(y < 1)(lambda: arrived("new1", new.at[1]))
    pl.when(y < 2)(lambda: arrived("new2", new.at[2]))
    arrived("new3", new.at[3])

    def padded(rows):
        return jnp.concatenate([rows, jnp.zeros((12,) + rows.shape[1:], F32)], axis=0).astype(BF16)

    d_normed = padded(norm(embedded, a_gain).astype(F32))
    dq = dot(d_normed, qkv_v[0]).astype(BF16).astype(F32)[0:4] * 0.125
    dk = dot(d_normed, qkv_v[1]).astype(BF16).astype(F32)[0:4]
    dv = dot(d_normed, qkv_v[2]).astype(BF16).astype(F32)[0:4]
    lane4 = lax.broadcasted_iota(jnp.int32, (4, 128), 1)
    qd8 = jnp.concatenate(
        [jnp.where(lane4 < 64, dq, 0.0), jnp.where(lane4 >= 64, dq, 0.0)], axis=0)
    qd16 = jnp.concatenate([qd8, jnp.zeros((8, 128), F32)], axis=0).astype(BF16)
    k_ids = jnp.concatenate(new_ids + past_ids, axis=1)
    rid = (lax.broadcasted_iota(jnp.int32, (16, 1024), 0) % 4).astype(F32)
    s = jnp.concatenate([dot_nt(qd16, block(b)[0:128, :]) for b in range(8)], axis=1)
    s = jnp.where(rid == k_ids, s, NEG)
    m = jnp.maximum(jnp.max(s, axis=1, keepdims=True), FLOOR)
    w = jnp.exp(s - m)
    l = jnp.sum(w, axis=1, keepdims=True)
    w = w.astype(BF16)
    o = sum(
        dot_nt(w[:, b * 128 : (b + 1) * 128], block(b)[128:256, :]) for b in range(8))
    dbuf[0, 0:8, :] = o[0:8]
    dbuf[0, 8:16, :] = jnp.broadcast_to(m[0:8], (8, 128))
    dbuf[0, 16:24, :] = jnp.broadcast_to(l[0:8], (8, 128))
    for g in z_order:
        remote("dpart", dbuf.at[0], dbuf.at[g], zpeer(g)).start()

    arrived("wo", wo_full.at[pl.ds(0, 3), 0])
    arrived("wof", wo_full.at[pl.ds(0, 3), 0])
    loads["wo"].wait()
    remote("swap", wo_full.at[:, core], wo_full.at[:, core], zpeer(1)).start()

    half = (pl.ds(0, 256), pl.ds(256, 256), pl.ds(512, 256), pl.ds(768, 256))
    def hidden_of(rows):
        gate = dot_nt(rows, ffn_v[0])
        up = dot_nt(rows, ffn_v[1])
        return (jax.nn.gelu(gate, approximate=True) * up).astype(BF16)

    def units(rows):
        return dot(hidden_of(rows), ffn_v[2])

    arrived("swap", wo_full.at[:, 0])
    arrived("att", abuf.at[:, pl.ds(0, 896)])
    residual = x_v[...].astype(F32) + dot(abuf[...], wo_full[...].reshape(1024, 1024))
    res_s[...] = residual

    own_m = jnp.sum(qd8 * jnp.concatenate([dk, dk], axis=0), axis=1, keepdims=True)
    own_m = jnp.broadcast_to(own_m, (8, 128))
    arrived("dpart", dbuf.at[pl.ds(1, 3)])
    dparts = [dbuf[e] for e in range(4)]
    joint = own_m
    for part in dparts:
        joint = jnp.maximum(joint, part[8:16])
    own_scale = jnp.exp(own_m - joint)
    weight = own_scale
    summed = own_scale * jnp.concatenate([dv, dv], axis=0)
    for part in dparts:
        scale = jnp.exp(part[8:16] - joint)
        weight = weight + scale * part[16:24]
        summed = summed + scale * part[0:8]
    summed = summed / weight
    d_attended = jnp.where(lane4 < 64, summed[0:4], summed[4:8])
    dabuf[t] = d_attended.astype(BF16)
    for r in t_order:
        remote("datt", dabuf.at[t], dabuf.at[t], tpeer(r)).start()

    loads["fg"].wait()
    f_gain = gain_of(fg_v)
    nbuf[...] = norm(residual, f_gain)
    loads["wg"].wait()
    loads["wu"].wait()
    loads["wd"].wait()
    hidden = hidden_of(nbuf[...])
    for h in range(4):
        part_s[:, half[h]] = dot(hidden, ffn_v[2, :, half[h]]).astype(BF16)
        for r in t_order:
            remote("rs2" + "abcd"[h], part_s.at[rows_of(r), half[h]], rs2buf.at[r, :, half[h]],
                   tpeer(r)).start()

    arrived("datt", dabuf.at[pl.ds(0, 7)])
    d_all = jnp.concatenate([dabuf[i].astype(F32) for i in range(8)], axis=1)
    d_residual = embedded + dot(padded(d_all), wo_full[...].reshape(1024, 1024))[0:4]
    ar2buf[0] = units(padded(norm(d_residual, f_gain).astype(F32)))[0:4].astype(BF16)
    for r in t_order:
        remote("ar2", ar2buf.at[0], ar2buf.at[r], tpeer(r)).start()

    for h in range(4):
        final = res_s[my_rows, half[h]] + part_s[my_rows, half[h]].astype(F32)
        arrived("rs2" + "abcd"[h], rs2buf.at[pl.ds(1, 7), :, half[h]])
        for r in range(1, 8):
            final = final + rs2buf[r, :, half[h]].astype(F32)
        out_ref[my_rows, half[h]] = final.astype(BF16)
        for r in t_order:
            remote("ag2", out_ref.at[my_rows, half[h]], out_ref.at[my_rows, half[h]],
                   tpeer(r)).start()

    arrived("ar2", ar2buf.at[pl.ds(1, 7)])
    d_final = d_residual + sum(ar2buf[r].astype(F32) for r in range(8))
    loads["lg"].wait()
    loads["lm"].wait()
    l_normed = padded(norm(d_final, gain_of(lg_v)).astype(F32))
    logits_ref[...] = dot(l_normed, lm_v[...])[0:4]

    arrived("relk", relk_ref.at[:, pl.ds(0, 896)])
    arrived("relv", relv_ref.at[:, pl.ds(0, 896)])
    for d in range(1, 4):
        sent("new%d" % d, new.at[d])
    sent("past", past.at[pl.ds(1, 3)])
    sent("ids", idall.at[pl.ds(1, 6)])
    sent("q", qbuf.at[pl.ds(1, 3)])
    sent("e1", e1buf.at[pl.ds(1, 7)])
    sent("e2", e2buf.at[pl.ds(1, 15)])
    sent("relk", relk_ref.at[:, pl.ds(0, 896)])
    sent("relv", relv_ref.at[:, pl.ds(0, 896)])
    sent("part", obuf.at[pl.ds(1, 3)])
    sent("stats", stbuf.at[pl.ds(1, 3)])
    sent("dpart", dbuf.at[pl.ds(1, 3)])
    sent("wo", wo_full.at[pl.ds(0, 3), 0])
    sent("woz", wo_full.at[0, 0])
    sent("wof", wo_full.at[pl.ds(0, 3), 0])
    sent("swap", wo_full.at[:, 0])
    sent("att", abuf.at[:, pl.ds(0, 896)])
    sent("datt", dabuf.at[pl.ds(0, 7)])
    sent("rs2a", rs2buf.at[pl.ds(1, 7), :, half[0]])
    sent("rs2b", rs2buf.at[pl.ds(1, 7), :, half[1]])
    sent("rs2c", rs2buf.at[pl.ds(1, 7), :, half[2]])
    sent("rs2d", rs2buf.at[pl.ds(1, 7), :, half[3]])
    sent("ar2", ar2buf.at[pl.ds(1, 7)])
    arrived("ag2", out_ref.at[pl.ds(0, 112)])
    sent("ag2", out_ref.at[pl.ds(0, 112)])


def hand_over(*refs):
    sems = refs[8]
    copies = [pltpu.make_async_copy(refs[i], refs[4 + i], sems.at[i]) for i in range(4)]
    for copy in copies:
        copy.start()
    for copy in copies:
        copy.wait()


def on_device(
    prompt_states, segment_ids, past_keys, past_values, cache_request, decode_ids, embed_table,
    attn_gain, ff_gain, final_gain, w_query, w_key, w_value, w_out, w_gate, w_up, w_down, lm_head,
):
    in_hbm = pl.BlockSpec(memory_space=pltpu.HBM)
    in_vmem = pl.BlockSpec(memory_space=pltpu.VMEM)
    dma = pltpu.SemaphoreType.DMA
    local = [
        ((128, 1024), BF16), ((1024,), BF16), ((1024,), BF16), ((1024,), BF16),
        ((3, 1024, 128), BF16), ((3, 352, 1024), BF16), ((1024, 251), BF16),
        ((251, 1024), BF16), ((128, 128), BF16),
        ((128, 128), BF16), ((8, 128, 128), F32), ((1024, 256), F32), ((8, 256), F32),
        ((8, 256), F32), ((128, 256), F32), ((4, 128, 128), BF16), ((4, 8, 128), F32),
        ((128, 1024), BF16), ((128, 1024), BF16), ((128, 1024), F32),
    ]
    arriving = [
        ((4, 256, 128), BF16), ((4, 256, 128), BF16), ((8, 8, 128), jnp.int32),
        ((4, 128, 128), BF16), ((4, 128, 128), BF16), ((4, 8, 128), F32), ((4, 24, 128), F32),
        ((8, 4, 1024), BF16), ((16, 4, 1024), BF16), ((4, 4, 1024), BF16),
        ((8, 2, 64, 1024), BF16), ((128, 1024), BF16), ((8, 4, 128), BF16),
        ((8, 16, 1024), BF16), ((8, 4, 1024), BF16),
    ]
    shapes = [((128, 1024), BF16), ((4, 251), F32), ((16, 1024), BF16), ((16, 1024), BF16)]
    arrays = [
        pltpu.with_memory_space_constraint(a, pltpu.HBM)
        for a in (
            prompt_states, segment_ids, past_keys, past_values, cache_request, embed_table,
            attn_gain, ff_gain, final_gain, w_query, w_key, w_value, w_out, w_gate.T, w_up.T,
            w_down, lm_head,
        )
    ]
    results = pl.pallas_call(
        kernel,
        out_shape=tuple(pltpu.VMEM(s, d) for s, d in shapes),
        in_specs=[pl.BlockSpec(memory_space=pltpu.SMEM)] + [in_hbm] * 17,
        out_specs=(in_vmem,) * 4,
        scratch_shapes=[pltpu.VMEM(s, d) for s, d in local + arriving]
        + [dma((17,)), dma((26,)), dma((26,))],
        compiler_params=pltpu.CompilerParams(
            collective_id=0, has_side_effects=True, vmem_limit_bytes=60 * 1024 * 1024),
    )(decode_ids, *arrays)
    results = [pltpu.with_memory_space_constraint(a, pltpu.VMEM) for a in results]
    return pl.pallas_call(
        hand_over,
        out_shape=tuple(jax.ShapeDtypeStruct(s, d) for s, d in shapes),
        in_specs=[in_vmem] * 4,
        out_specs=(in_hbm,) * 4,
        scratch_shapes=[dma((4,))],
    )(*results)


def solution(mesh):
    placed = (
        P("ctx", None),
        P("ctx"),
        P("ctx", "tp"),
        P("ctx", "tp"),
        P("ctx"),
        P(),
        P(("ctx", "tp"), None),
        P(),
        P(),
        P(),
        P(None, "tp"),
        P(None, "tp"),
        P(None, "tp"),
        P("tp", None),
        P(None, "tp"),
        P(None, "tp"),
        P("tp", None),
        P(None, ("ctx", "tp")),
    )
    return jax.shard_map(
        on_device,
        mesh=mesh,
        in_specs=placed,
        out_specs=(
            P("ctx", None),
            P(None, ("ctx", "tp")),
            P(("ctx", "tp"), None),
            P(("ctx", "tp"), None),
        ),
        check_vma=False,
    )
```

```python
import jax
import jax.numpy as jnp
from jax import lax
from jax.experimental import pallas as pl
from jax.experimental.pallas import tpu as pltpu
from jax.sharding import PartitionSpec as P

DH = 64
EPS = 1e-06
NEG = -1e30
FLOOR = -1e29
MESH = pl.DeviceIdType.MESH
F32 = jnp.float32
BF16 = jnp.bfloat16


def dot(a, b):
    return jnp.dot(a, b, preferred_element_type=F32)


def dot_nt(a, b):
    return lax.dot_general(a, b, (((1,), (1,)), ((), ())), preferred_element_type=F32)


def norm(states, gain):
    mean_square = jnp.mean(states * states, axis=-1, keepdims=True)
    return (states * lax.rsqrt(mean_square + EPS) * gain).astype(BF16)


def kernel(
    ids_ref, x_hbm, seg_hbm, pk_hbm, pv_hbm, creq_hbm, emb_hbm,
    ag_hbm, fg_hbm, lg_hbm, wq_hbm, wk_hbm, wv_hbm, wo_hbm, wg_hbm, wu_hbm, wd_hbm, lm_hbm,
    out_ref, logits_ref, relk_ref, relv_ref,
    x_v, ag_v, fg_v, lg_v, qkv_v, ffn_v, lm_v, emb_v, pv_v,
    vrow, kid_s, s_s, hi_s, tw_s, o_s, osend, stsend, part_s, nbuf, res_s,
    past, new, idall, qbuf, obuf, stbuf, dbuf, e1buf, e2buf, e3buf,
    wo_full, abuf, dabuf, rs2buf, ar2buf,
    lsem, ssem, rsem,
):
    c = lax.axis_index("ctx")
    t = lax.axis_index("tp")
    y = lax.div(c, 4)
    zc = lax.rem(c, 4)
    z_hi = lax.div(zc, 2)
    core = lax.rem(c, 2)
    z_lo = lax.div(t, 4)
    x = lax.rem(t, 4)

    def ypeer(d):
        return (lax.rem(y + d, 4) * 4 + zc, t)

    def zc_of(g):
        return lax.rem(z_hi + lax.div(g, 2), 2) * 2 + lax.rem(core + lax.rem(g, 2), 2)

    def zpeer(g):
        return (y * 4 + zc_of(jnp.int32(g)), t)

    def t_of(r):
        return lax.rem(z_lo + r // 4, 2) * 4 + lax.rem(x + r % 4, 4)

    def tpeer(r):
        return (c, t_of(r))

    def cpeer(k):
        return (lax.rem(y + k // 4, 4) * 4 + zc_of(jnp.int32(k % 4)), t)

    c_order = (11, 10, 7, 15, 6, 14, 9, 8, 3, 2, 5, 13, 4, 12, 1)
    y_order = (2, 1, 3)
    z_order = (3, 2, 1)
    t_order = (6, 5, 7, 2, 4, 1, 3)

    names = (
        "past", "new1", "new2", "new3", "ids", "q", "e1", "e2", "e3", "relk", "relv",
        "part", "stats", "dpart", "wo", "woz", "wof", "swap", "swap2", "att", "datt", "rs2a", "rs2b", "rs2c", "rs2d", "ar2", "ag2",
    )

    def remote(name, src, dst, peer):
        at = names.index(name)
        return pltpu.make_async_remote_copy(
            src_ref=src, dst_ref=dst, send_sem=ssem.at[at], recv_sem=rsem.at[at],
            device_id=peer, device_id_type=MESH,
        )

    def arrived(name, whole):
        remote(name, whole, whole, tpeer(1)).wait_recv()

    def sent(name, whole):
        remote(name, whole, whole, tpeer(1)).wait_send()

    barrier = pltpu.get_barrier_semaphore()
    for r in range(1, 4):
        pl.semaphore_signal(barrier, 1, device_id=ypeer(r), device_id_type=MESH)
    for r in range(1, 4):
        pl.semaphore_signal(barrier, 1, device_id=zpeer(r), device_id_type=MESH)
    for r in range(1, 8):
        pl.semaphore_signal(barrier, 1, device_id=tpeer(r), device_id_type=MESH)

    my_half = pl.ds(pl.multiple_of(core * 64, 64), 64)
    loads = {}
    todo = [
        ("x", x_hbm, x_v), ("ag", ag_hbm, ag_v),
        ("wk", wk_hbm, qkv_v.at[1]), ("wv", wv_hbm, qkv_v.at[2]), ("wq", wq_hbm, qkv_v.at[0]),
        ("pk", pk_hbm, past.at[0, pl.ds(0, 128)]), ("pv", pv_hbm, pv_v),
        ("seg", seg_hbm, idall.at[0, 0]), ("creq", creq_hbm, idall.at[0, 1]),
        ("emb", emb_hbm, emb_v), ("wo", wo_hbm.at[my_half], wo_full.at[t, core]), ("fg", fg_hbm, fg_v),
        ("wg", wg_hbm, ffn_v.at[0]), ("wu", wu_hbm, ffn_v.at[1]), ("wd", wd_hbm, ffn_v.at[2]),
        ("lg", lg_hbm, lg_v), ("lm", lm_hbm, lm_v),
    ]
    for i, (name, src, dst) in enumerate(todo):
        loads[name] = pltpu.make_async_copy(src, dst, lsem.at[i])
        loads[name].start()

    def gain_of(ref):
        return ref[...].astype(F32).reshape(1, 1024)

    loads["x"].wait()
    loads["ag"].wait()
    a_gain = gain_of(ag_v)
    normed = norm(x_v[...].astype(F32), a_gain)
    loads["wk"].wait()
    new[0, 0:128, :] = dot(normed, qkv_v[1]).astype(BF16)
    loads["wv"].wait()
    values = dot(normed, qkv_v[2])
    vrow[...] = values.astype(BF16)
    new[0, 128:256, :] = values.T.astype(BF16)
    loads["wq"].wait()
    queries = dot(normed, qkv_v[0]).astype(BF16).astype(F32) * 0.125
    qbuf[0] = queries.T.astype(BF16)
    loads["pk"].wait()
    loads["pv"].wait()
    past[0, 128:256, :] = pv_v[...].astype(F32).T.astype(BF16)
    loads["seg"].wait()
    loads["creq"].wait()

    first_row = (c * 8 + t) * 251
    row16 = lax.broadcasted_iota(jnp.int32, (16, 251), 0)
    col16 = lax.broadcasted_iota(jnp.int32, (16, 251), 1) + first_row
    wanted = jnp.full((16, 251), -1, jnp.int32)
    for q in range(4):
        wanted = jnp.where(row16 == q, ids_ref[q], wanted)
    one_hot = (col16 == wanted).astype(F32).astype(BF16)
    loads["emb"].wait()
    e1buf[0] = dot(one_hot, emb_v[...])[0:4].astype(BF16)
    pl.semaphore_wait(barrier, 13)

    for r in t_order:
        remote("e1", e1buf.at[0], e1buf.at[r], tpeer(r)).start()

    def send_new(d):
        remote("new%d" % d, new.at[0], new.at[d], ypeer(d)).start()

    for d in (2, 1):
        pl.when(y + d < 4)(lambda d=d: send_new(d))
    for g in z_order:
        remote("q", qbuf.at[0], qbuf.at[g], zpeer(g)).start()
    for d in y_order:
        remote("past", past.at[0], past.at[d], ypeer(d)).start()
    for d in y_order:
        remote("ids", idall.at[0], idall.at[d], ypeer(d)).start()
    for g in z_order:
        remote("ids", idall.at[0], idall.at[3 + g], zpeer(g)).start()

    remote("woz", wo_hbm.at[my_half], wo_full.at[t, core], tpeer(4)).start()
    for r in (2, 1, 3):
        remote("wo", wo_hbm.at[my_half], wo_full.at[t, core], tpeer(r)).start()

    my_columns = pl.ds(pl.multiple_of(t * 128, 128), 128)
    my_rows = pl.ds(pl.multiple_of(t * 16, 16), 16)

    def rows_of(r):
        return pl.ds(pl.multiple_of(t_of(r) * 16, 16), 16)

    for d in (2, 1):
        pl.when(y + d >= 4)(lambda d=d: send_new(d))
    send_new(3)
    for r in t_order:
        remote("relk", new.at[0, rows_of(r)], relk_ref.at[:, my_columns], tpeer(r)).start()
        remote("relv", vrow.at[rows_of(r)], relv_ref.at[:, my_columns], tpeer(r)).start()
    relk_ref[:, my_columns] = new[0, my_rows, :]
    relv_ref[:, my_columns] = vrow[my_rows, :]

    arrived("woz", wo_full.at[0, 0])
    across = t_of(4)
    for r in (2, 1, 3):
        remote("wof", wo_full.at[across, core], wo_full.at[across, core], tpeer(r)).start()

    arrived("ids", idall.at[pl.ds(1, 6)])
    new_ids = [idall[d, 0:1, :].astype(F32) for d in range(4)]
    past_ids = [idall[d, 1:2, :].astype(F32) for d in range(4)]
    id_columns = jnp.concatenate(
        new_ids + past_ids + [jnp.zeros((120, 128), F32)], axis=0).T
    for b in range(8):
        kid_s[b] = jnp.broadcast_to(id_columns[:, b : b + 1], (128, 128))
    idall[7] = idall[0]
    arrived("q", qbuf.at[pl.ds(1, 3)])
    arrived("e1", e1buf.at[pl.ds(1, 7)])
    e2buf[0] = sum(e1buf[r].astype(F32) for r in range(8)).astype(BF16)
    for k in c_order:
        remote("e2", e2buf.at[0], e2buf.at[k], cpeer(k)).start()

    pl.when(y >= 1)(lambda: arrived("new1", new.at[1]))
    pl.when(y >= 2)(lambda: arrived("new2", new.at[2]))
    arrived("past", past.at[pl.ds(1, 3)])

    def block(b):
        return new.at[b] if b < 4 else past.at[b - 4]

    k_iota = lax.broadcasted_iota(jnp.int32, (128, 128), 0)
    q_iota = lax.broadcasted_iota(jnp.int32, (128, 128), 1)

    def attend(i, _):
        g = 3 - i
        qt = qbuf[g]
        top = qt[0:64, :]
        low = qt[64:128, :]
        zero = jnp.zeros((64, 128), BF16)
        qd = jnp.concatenate(
            [jnp.concatenate([top, zero], axis=1), jnp.concatenate([zero, low], axis=1)], axis=0)
        qid = idall[4 + lax.rem(g + 3, 4), 0:1, :].astype(F32)
        q_at = y * 512 + zc_of(g) * 128

        def score(b):
            s = dot(block(b)[0:128, :], qd)
            ok = kid_s[b] == qid
            if b < 4:
                k_at = (y - b) * 512 + zc * 128
                ok = ok & (k_iota + (k_at - q_at) <= q_iota)
            s = jnp.where(jnp.concatenate([ok, ok], axis=1), s, NEG)
            s_s[b * 128 : (b + 1) * 128, :] = s
            return jnp.max(s.reshape(16, 8, 256), axis=0)

        def weigh(b, m):
            w = jnp.exp(s_s[b * 128 : (b + 1) * 128, :] - m)
            return jnp.sum(w.reshape(16, 8, 256), axis=0), dot(
                block(b)[128:256, :], w.astype(BF16))

        always = (0, 4, 5, 6, 7)
        highest = jnp.full((8, 256), FLOOR, F32)
        for b in always:
            highest = jnp.maximum(highest, score(b))
        hi_s[...] = highest

        def score_more(b):
            hi_s[...] = jnp.maximum(hi_s[...], score(b))

        pl.when(y >= 1)(lambda: score_more(1))
        pl.when(y >= 2)(lambda: score_more(2))
        m = jnp.max(hi_s[...], axis=0, keepdims=True)
        total_w = jnp.zeros((8, 256), F32)
        o = jnp.zeros((128, 256), F32)
        for b in always:
            more_w, more_o = weigh(b, m)
            total_w = total_w + more_w
            o = o + more_o
        tw_s[...] = total_w
        o_s[...] = o

        def weigh_more(b):
            more_w, more_o = weigh(b, m)
            tw_s[...] += more_w
            o_s[...] += more_o

        pl.when(y >= 1)(lambda: weigh_more(1))
        pl.when(y >= 2)(lambda: weigh_more(2))
        l = jnp.sum(tw_s[...], axis=0, keepdims=True)
        osend[g] = jnp.concatenate(
            [o_s[0:64, 0:128], o_s[64:128, 128:256]], axis=0).astype(BF16)
        stsend[g] = jnp.concatenate(
            [m[:, 0:128], m[:, 128:256], l[:, 0:128], l[:, 128:256], jnp.zeros((4, 128), F32)],
            axis=0)

        @pl.when(i < 3)
        def _():
            remote("part", osend.at[g], obuf.at[g], zpeer(g)).start()
            remote("stats", stsend.at[g], stbuf.at[g], zpeer(g)).start()

        return 0

    lax.fori_loop(0, 4, attend, 0)
    obuf[0] = osend[0]
    stbuf[0] = stsend[0]

    near = pl.ds(z_lo * 4, 4)
    far = pl.ds((1 - z_lo) * 4, 4)
    arrived("wo", wo_full.at[pl.ds(0, 3), 0])
    loads["wo"].wait()
    remote("swap", wo_full.at[near, core], wo_full.at[near, core], zpeer(1)).start()

    arrived("part", obuf.at[pl.ds(1, 3)])
    arrived("stats", stbuf.at[pl.ds(1, 3)])
    stats = [stbuf[f] for f in range(4)]
    tops = [st[0:2] for st in stats]
    joint = jnp.maximum(jnp.maximum(tops[0], tops[1]), jnp.maximum(tops[2], tops[3]))
    scales = [jnp.exp(m - joint) for m in tops]
    weight = sum(sc * st[2:4] for sc, st in zip(scales, stats))
    inverse = 1.0 / weight
    attended = jnp.zeros((128, 128), F32)
    for f in range(4):
        factor = scales[f] * inverse
        spread = jnp.concatenate(
            [jnp.broadcast_to(factor[0:1], (64, 128)), jnp.broadcast_to(factor[1:2], (64, 128))],
            axis=0)
        attended = attended + obuf[f].astype(F32) * spread
    abuf[:, my_columns] = attended.T.astype(BF16)
    for r in t_order:
        remote("att", abuf.at[:, my_columns], abuf.at[:, my_columns], tpeer(r)).start()

    arrived("e2", e2buf.at[pl.ds(1, 15)])
    embedded = sum(e2buf[k].astype(F32) for k in range(16))
    pl.when(y < 1)(lambda: arrived("new1", new.at[1]))
    pl.when(y < 2)(lambda: arrived("new2", new.at[2]))
    arrived("new3", new.at[3])

    def padded(rows):
        return jnp.concatenate([rows, jnp.zeros((12,) + rows.shape[1:], F32)], axis=0).astype(BF16)

    d_normed = padded(norm(embedded, a_gain).astype(F32))
    dq = dot(d_normed, qkv_v[0]).astype(BF16).astype(F32)[0:4] * 0.125
    dk = dot(d_normed, qkv_v[1]).astype(BF16).astype(F32)[0:4]
    dv = dot(d_normed, qkv_v[2]).astype(BF16).astype(F32)[0:4]
    lane4 = lax.broadcasted_iota(jnp.int32, (4, 128), 1)
    qd8 = jnp.concatenate(
        [jnp.where(lane4 < 64, dq, 0.0), jnp.where(lane4 >= 64, dq, 0.0)], axis=0)
    qd16 = jnp.concatenate([qd8, jnp.zeros((8, 128), F32)], axis=0).astype(BF16)
    k_ids = jnp.concatenate(new_ids + past_ids, axis=1)
    rid = (lax.broadcasted_iota(jnp.int32, (16, 1024), 0) % 4).astype(F32)
    s = jnp.concatenate([dot_nt(qd16, block(b)[0:128, :]) for b in range(8)], axis=1)
    s = jnp.where(rid == k_ids, s, NEG)
    m = jnp.maximum(jnp.max(s, axis=1, keepdims=True), FLOOR)
    w = jnp.exp(s - m)
    l = jnp.sum(w, axis=1, keepdims=True)
    w = w.astype(BF16)
    o = sum(
        dot_nt(w[:, b * 128 : (b + 1) * 128], block(b)[128:256, :]) for b in range(8))
    dbuf[0, 0:8, :] = o[0:8]
    dbuf[0, 8:16, :] = jnp.broadcast_to(m[0:8], (8, 128))
    dbuf[0, 16:24, :] = jnp.broadcast_to(l[0:8], (8, 128))
    for g in z_order:
        remote("dpart", dbuf.at[0], dbuf.at[g], zpeer(g)).start()

    arrived("wof", wo_full.at[pl.ds(0, 3), 0])
    remote("swap2", wo_full.at[far, core], wo_full.at[far, core], zpeer(1)).start()

    half = (pl.ds(0, 256), pl.ds(256, 256), pl.ds(512, 256), pl.ds(768, 256))
    def hidden_of(rows):
        gate = dot_nt(rows, ffn_v[0])
        up = dot_nt(rows, ffn_v[1])
        return (jax.nn.gelu(gate, approximate=True) * up).astype(BF16)

    def units(rows):
        return dot(hidden_of(rows), ffn_v[2])

    arrived("swap", wo_full.at[pl.ds(0, 4), 0])
    arrived("att", abuf.at[:, pl.ds(0, 896)])
    near_lanes = pl.ds(pl.multiple_of(z_lo * 512, 512), 512)
    far_lanes = pl.ds(pl.multiple_of((1 - z_lo) * 512, 512), 512)
    residual = x_v[...].astype(F32) + dot(
        abuf[:, near_lanes], wo_full[near].reshape(512, 1024))
    arrived("swap2", wo_full.at[pl.ds(0, 4), 0])
    residual = residual + dot(abuf[:, far_lanes], wo_full[far].reshape(512, 1024))
    res_s[...] = residual

    own_m = jnp.sum(qd8 * jnp.concatenate([dk, dk], axis=0), axis=1, keepdims=True)
    own_m = jnp.broadcast_to(own_m, (8, 128))
    arrived("dpart", dbuf.at[pl.ds(1, 3)])
    dparts = [dbuf[e] for e in range(4)]
    joint = own_m
    for part in dparts:
        joint = jnp.maximum(joint, part[8:16])
    own_scale = jnp.exp(own_m - joint)
    weight = own_scale
    summed = own_scale * jnp.concatenate([dv, dv], axis=0)
    for part in dparts:
        scale = jnp.exp(part[8:16] - joint)
        weight = weight + scale * part[16:24]
        summed = summed + scale * part[0:8]
    summed = summed / weight
    d_attended = jnp.where(lane4 < 64, summed[0:4], summed[4:8])
    dabuf[t] = d_attended.astype(BF16)
    for r in t_order:
        remote("datt", dabuf.at[t], dabuf.at[t], tpeer(r)).start()

    loads["fg"].wait()
    f_gain = gain_of(fg_v)
    nbuf[...] = norm(residual, f_gain)
    loads["wg"].wait()
    loads["wu"].wait()
    loads["wd"].wait()
    hidden = hidden_of(nbuf[...])
    for h in range(4):
        part_s[:, half[h]] = dot(hidden, ffn_v[2, :, half[h]]).astype(BF16)
        for r in t_order:
            remote("rs2" + "abcd"[h], part_s.at[rows_of(r), half[h]], rs2buf.at[r, :, half[h]],
                   tpeer(r)).start()

    arrived("datt", dabuf.at[pl.ds(0, 7)])
    d_all = jnp.concatenate([dabuf[i].astype(F32) for i in range(8)], axis=1)
    d_residual = embedded + dot(padded(d_all), wo_full[...].reshape(1024, 1024))[0:4]
    ar2buf[0] = units(padded(norm(d_residual, f_gain).astype(F32)))[0:4].astype(BF16)
    for r in t_order:
        remote("ar2", ar2buf.at[0], ar2buf.at[r], tpeer(r)).start()

    for h in range(4):
        final = res_s[my_rows, half[h]] + part_s[my_rows, half[h]].astype(F32)
        arrived("rs2" + "abcd"[h], rs2buf.at[pl.ds(1, 7), :, half[h]])
        for r in range(1, 8):
            final = final + rs2buf[r, :, half[h]].astype(F32)
        out_ref[my_rows, half[h]] = final.astype(BF16)
        for r in t_order:
            remote("ag2", out_ref.at[my_rows, half[h]], out_ref.at[my_rows, half[h]],
                   tpeer(r)).start()

    arrived("ar2", ar2buf.at[pl.ds(1, 7)])
    d_final = d_residual + sum(ar2buf[r].astype(F32) for r in range(8))
    loads["lg"].wait()
    loads["lm"].wait()
    l_normed = padded(norm(d_final, gain_of(lg_v)).astype(F32))
    logits_ref[...] = dot(l_normed, lm_v[...])[0:4]

    arrived("relk", relk_ref.at[:, pl.ds(0, 896)])
    arrived("relv", relv_ref.at[:, pl.ds(0, 896)])
    for d in range(1, 4):
        sent("new%d" % d, new.at[d])
    sent("past", past.at[pl.ds(1, 3)])
    sent("ids", idall.at[pl.ds(1, 6)])
    sent("q", qbuf.at[pl.ds(1, 3)])
    sent("e1", e1buf.at[pl.ds(1, 7)])
    sent("e2", e2buf.at[pl.ds(1, 15)])
    sent("relk", relk_ref.at[:, pl.ds(0, 896)])
    sent("relv", relv_ref.at[:, pl.ds(0, 896)])
    sent("part", obuf.at[pl.ds(1, 3)])
    sent("stats", stbuf.at[pl.ds(1, 3)])
    sent("dpart", dbuf.at[pl.ds(1, 3)])
    sent("wo", wo_full.at[pl.ds(0, 3), 0])
    sent("woz", wo_full.at[0, 0])
    sent("wof", wo_full.at[pl.ds(0, 3), 0])
    sent("swap", wo_full.at[pl.ds(0, 4), 0])
    sent("swap2", wo_full.at[pl.ds(0, 4), 0])
    sent("att", abuf.at[:, pl.ds(0, 896)])
    sent("datt", dabuf.at[pl.ds(0, 7)])
    sent("rs2a", rs2buf.at[pl.ds(1, 7), :, half[0]])
    sent("rs2b", rs2buf.at[pl.ds(1, 7), :, half[1]])
    sent("rs2c", rs2buf.at[pl.ds(1, 7), :, half[2]])
    sent("rs2d", rs2buf.at[pl.ds(1, 7), :, half[3]])
    sent("ar2", ar2buf.at[pl.ds(1, 7)])
    arrived("ag2", out_ref.at[pl.ds(0, 112)])
    sent("ag2", out_ref.at[pl.ds(0, 112)])


def hand_over(*refs):
    sems = refs[8]
    copies = [pltpu.make_async_copy(refs[i], refs[4 + i], sems.at[i]) for i in range(4)]
    for copy in copies:
        copy.start()
    for copy in copies:
        copy.wait()


def on_device(
    prompt_states, segment_ids, past_keys, past_values, cache_request, decode_ids, embed_table,
    attn_gain, ff_gain, final_gain, w_query, w_key, w_value, w_out, w_gate, w_up, w_down, lm_head,
):
    in_hbm = pl.BlockSpec(memory_space=pltpu.HBM)
    in_vmem = pl.BlockSpec(memory_space=pltpu.VMEM)
    dma = pltpu.SemaphoreType.DMA
    local = [
        ((128, 1024), BF16), ((1024,), BF16), ((1024,), BF16), ((1024,), BF16),
        ((3, 1024, 128), BF16), ((3, 352, 1024), BF16), ((1024, 251), BF16),
        ((251, 1024), BF16), ((128, 128), BF16),
        ((128, 128), BF16), ((8, 128, 128), F32), ((1024, 256), F32), ((8, 256), F32),
        ((8, 256), F32), ((128, 256), F32), ((4, 128, 128), BF16), ((4, 8, 128), F32),
        ((128, 1024), BF16), ((128, 1024), BF16), ((128, 1024), F32),
    ]
    arriving = [
        ((4, 256, 128), BF16), ((4, 256, 128), BF16), ((8, 8, 128), jnp.int32),
        ((4, 128, 128), BF16), ((4, 128, 128), BF16), ((4, 8, 128), F32), ((4, 24, 128), F32),
        ((8, 4, 1024), BF16), ((16, 4, 1024), BF16), ((4, 4, 1024), BF16),
        ((8, 2, 64, 1024), BF16), ((128, 1024), BF16), ((8, 4, 128), BF16),
        ((8, 16, 1024), BF16), ((8, 4, 1024), BF16),
    ]
    shapes = [((128, 1024), BF16), ((4, 251), F32), ((16, 1024), BF16), ((16, 1024), BF16)]
    arrays = [
        pltpu.with_memory_space_constraint(a, pltpu.HBM)
        for a in (
            prompt_states, segment_ids, past_keys, past_values, cache_request, embed_table,
            attn_gain, ff_gain, final_gain, w_query, w_key, w_value, w_out, w_gate.T, w_up.T,
            w_down, lm_head,
        )
    ]
    results = pl.pallas_call(
        kernel,
        out_shape=tuple(pltpu.VMEM(s, d) for s, d in shapes),
        in_specs=[pl.BlockSpec(memory_space=pltpu.SMEM)] + [in_hbm] * 17,
        out_specs=(in_vmem,) * 4,
        scratch_shapes=[pltpu.VMEM(s, d) for s, d in local + arriving]
        + [dma((17,)), dma((27,)), dma((27,))],
        compiler_params=pltpu.CompilerParams(
            collective_id=0, has_side_effects=True, vmem_limit_bytes=60 * 1024 * 1024),
    )(decode_ids, *arrays)
    results = [pltpu.with_memory_space_constraint(a, pltpu.VMEM) for a in results]
    return pl.pallas_call(
        hand_over,
        out_shape=tuple(jax.ShapeDtypeStruct(s, d) for s, d in shapes),
        in_specs=[in_vmem] * 4,
        out_specs=(in_hbm,) * 4,
        scratch_shapes=[dma((4,))],
    )(*results)


def solution(mesh):
    placed = (
        P("ctx", None),
        P("ctx"),
        P("ctx", "tp"),
        P("ctx", "tp"),
        P("ctx"),
        P(),
        P(("ctx", "tp"), None),
        P(),
        P(),
        P(),
        P(None, "tp"),
        P(None, "tp"),
        P(None, "tp"),
        P("tp", None),
        P(None, "tp"),
        P(None, "tp"),
        P("tp", None),
        P(None, ("ctx", "tp")),
    )
    return jax.shard_map(
        on_device,
        mesh=mesh,
        in_specs=placed,
        out_specs=(
            P("ctx", None),
            P(None, ("ctx", "tp")),
            P(("ctx", "tp"), None),
            P(("ctx", "tp"), None),
        ),
        check_vma=False,
    )
```
